256 devices in a mesh: dp: 16 (over z, core), mp: 16 (over y, x).
Axes of the slice: x: 4, y: 4, z: 8, core: 2. Of those that a mesh axis runs over, the one named last changes fastest.
Arguments:
- intermediate_signal: bfloat16 [16, 1024, 14336], P('mp', None, 'dp'), may hold values from -6 to 6
- frozen_down_weight: bfloat16 [14336, 4096], P('dp', 'mp'), may hold values from -0.046875 to 0.046875
- lowdim_entry_matrices: bfloat16 [16, 16, 14336, 64], P('mp', None, 'dp'), may hold values from -0.046875 to 0.046875
- lowdim_exit_matrices: bfloat16 [16, 16, 64, 4096], P('mp', 'dp'), may hold values from -0.75 to 0.75
- result_sensitivity: bfloat16 [16, 1024, 4096], P('mp', 'dp'), may hold values from -6 to 6
- token_client_choice: int32 [16, 1024], P('mp'), may hold values from 0 to 15, as said below
- matrix_bank_position: int32 [16, 16], P('mp'), may hold values from 0 to 15, as said below
- shard_active_entries: int32 [16, 16], P('mp'), may hold values from 32 to 64, as said below
Outputs:
- customized_projection_result: bfloat16 [16, 1024, 4096], P('mp', 'dp')
- entry_matrix_derivative: float32 [16, 16, 14336, 64], P('mp', None, 'dp')
- exit_matrix_derivative: float32 [16, 16, 64, 4096], P('mp', 'dp')
The draws below stay inside these ranges and needn't reach their ends.
Inputs may be any that keep to these rules, and one draw needn't show every extreme that they name: `token_client_choice`: rows s * 64 to (s + 1) * 64 - 1 of a group belong to device s of dp. The owner of adapter u is matrix_bank_position[u]. Of one device's live rows at most 8 have adapters of one owner, and in every group one owner gets exactly 8 live rows from every device. `matrix_bank_position`: in each group a permutation of the slots. The live rows of a device are its first shard_active_entries rows; in each group some device has 64.
All inputs are finite; a program needn't handle non-finite values.
Results may differ from the reference program's by a relative error of at most 0.0065.
Values may be sent and summed in bfloat16 or wider, within the bound.
A program may use at most 128 MiB of HBM per device.

```python
import jax
import jax.numpy as jnp
from jax import lax

OUTPUT_FEATURES = 4096
HIDDEN_UNITS = 14336
ADAPTER_RANK = 64
TOK_DEV = 64
AD_DEV = 1
CAP = 8
REQUEST_GROUPS = 16
ROWS = 1024
GROUP_ADAPTERS = 16
N_DP = 16


def routing(key):

    def single_group(group_key):
        keys = jax.random.split(group_key, 8)
        slots = jax.random.permutation(keys[0], GROUP_ADAPTERS).astype(jnp.int32)
        inverse = jnp.argsort(slots).astype(jnp.int32)
        hot_owner = jax.random.randint(keys[1], (), 0, N_DP)
        counts = jax.random.randint(keys[2], (N_DP,), TOK_DEV // 2, TOK_DEV + 1)
        full_device = jax.random.randint(keys[3], (), 0, N_DP)
        counts = jnp.where(jnp.arange(N_DP) == full_device, TOK_DEV, counts).astype(jnp.int32)
        position = jnp.arange(TOK_DEV, dtype=jnp.int32)
        is_live = position[None, :] < counts[:, None]
        scores = jax.random.randint(keys[4], (N_DP, TOK_DEV), 0, 1 << 20) * TOK_DEV + position[None, :]
        scores = jnp.where(is_live, scores, (1 << 30) + position[None, :])
        row_order = jnp.argsort(scores, axis=1)
        sequence = jnp.argsort(row_order, axis=1)
        offset = jax.random.randint(keys[5], (N_DP, 1), 0, N_DP - 1)
        others = (hot_owner + 1 + (sequence - CAP + offset) % (N_DP - 1)) % N_DP
        owners = jnp.where(sequence < CAP, hot_owner, others)
        local_slot = jax.random.randint(keys[6], (N_DP, TOK_DEV), 0, AD_DEV)
        chosen = inverse[owners * AD_DEV + local_slot]
        spare_ids = jax.random.randint(keys[7], (N_DP, TOK_DEV), 0, GROUP_ADAPTERS)
        adapter_ids = jnp.where(is_live, chosen, spare_ids).astype(jnp.int32).reshape(ROWS)
        return (adapter_ids, slots, counts)
    group_keys = jax.random.split(jax.random.fold_in(key, 7), REQUEST_GROUPS)
    return jax.vmap(single_group)(group_keys)


def draw_token_client_choice(key, part):
    return routing(key)[0]


def draw_matrix_bank_position(key, part):
    return routing(key)[1]


def draw_shard_active_entries(key, part):
    return routing(key)[2]


def spiked(result, own_key, source, target, parts, factor):
    def block_of(axis_at):
        return (jnp.arange(result.shape[axis_at]) // (result.shape[axis_at] // parts)).reshape((-1,) + (1,) * (result.ndim - 1 - axis_at))

    one_side = jax.random.permutation(own_key, parts)[block_of(target)]
    second = (block_of(target) + parts // 2) % parts
    return jnp.where((block_of(source) == one_side) | (block_of(source) == second), factor * result, result)


def steps_of(key, shape, shards, least, high):
    def one(axis_at, shards_of):
        steps = jax.random.uniform(jax.random.fold_in(jax.random.fold_in(key, 6), axis_at), (shards_of,), jnp.float32, least / len(shards), high / len(shards))
        return jnp.repeat(jnp.exp(steps), shape[axis_at] // shards_of).reshape((-1,) + (1,) * (len(shape) - axis_at - 1))

    level = one(*shards[0])
    for cut in shards[1:]:
        level = level * one(*cut)
    return level


def bell_draw(rng, dims, spread, limit, cuts=(), held_as=jnp.bfloat16):
    gain = steps_of(rng, dims, cuts, -0.22, 0.18) if cuts else 1.0
    result = jax.random.normal(rng, dims, jnp.float32) * spread * gain
    return jnp.minimum(jnp.maximum(result, -limit), limit).astype(held_as)


def bell_draw_with(stream_key, dims, scale, bound, cuts, heavy, kind=jnp.bfloat16):
    entries = scale * jax.random.normal(stream_key, dims, jnp.float32)
    if cuts:
        entries = entries * steps_of(stream_key, dims, cuts, -0.22, 0.18)
    return jnp.clip(spiked(entries, jax.random.fold_in(stream_key, 3), *heavy), -bound, bound).astype(kind)


def setup_inputs(seed: int = 0) -> dict:
    arg_keys = jax.random.split(jax.random.key(seed), 9)
    intermediate_signal = bell_draw_with(arg_keys[0], (REQUEST_GROUPS, ROWS, HIDDEN_UNITS), 1.0, 6.0, ((0, 16), (2, 16)), (2, 1, 16, 2.0))
    frozen_down_weight = bell_draw(arg_keys[1], (HIDDEN_UNITS, OUTPUT_FEATURES), HIDDEN_UNITS ** -0.5, 0.046875, ((0, 16), (1, 16)))
    lowdim_entry_matrices = bell_draw(arg_keys[2], (REQUEST_GROUPS, GROUP_ADAPTERS, HIDDEN_UNITS, ADAPTER_RANK), HIDDEN_UNITS ** -0.5, 0.046875, ((0, 16), (2, 16)))
    lowdim_exit_matrices = bell_draw(arg_keys[3], (REQUEST_GROUPS, GROUP_ADAPTERS, ADAPTER_RANK, OUTPUT_FEATURES), ADAPTER_RANK ** -0.5, 0.75, ((0, 16), (1, 16)))
    result_sensitivity = bell_draw(arg_keys[4], (REQUEST_GROUPS, ROWS, OUTPUT_FEATURES), 1.0, 6.0, ((0, 16), (1, 16)))
    token_client_choice = draw_token_client_choice(jax.random.fold_in(arg_keys[8], 71), 0)
    matrix_bank_position = draw_matrix_bank_position(jax.random.fold_in(arg_keys[8], 71), 0)
    shard_active_entries = draw_shard_active_entries(jax.random.fold_in(arg_keys[8], 71), 0)
    return dict(intermediate_signal=intermediate_signal, frozen_down_weight=frozen_down_weight, lowdim_entry_matrices=lowdim_entry_matrices, lowdim_exit_matrices=lowdim_exit_matrices, result_sensitivity=result_sensitivity, token_client_choice=token_client_choice, matrix_bank_position=matrix_bank_position, shard_active_entries=shard_active_entries)


def single_group(intermediate_signal, frozen_down_weight, lowdim_entry_matrices, lowdim_exit_matrices, result_sensitivity, token_client_choice, matrix_bank_position, shard_active_entries):
    row_total = intermediate_signal.shape[0]
    adapter_list = lowdim_entry_matrices.shape[0]
    row_ids = jnp.arange(row_total, dtype=jnp.int32)
    is_live = (row_ids % TOK_DEV) < shard_active_entries[row_ids // TOK_DEV]
    storage = matrix_bank_position[token_client_choice]
    choose = ((storage[:, None] == jnp.arange(adapter_list, dtype=jnp.int32)[None, :]) & is_live[:, None]).astype(jnp.float32)
    base_term = jnp.dot(intermediate_signal, frozen_down_weight, preferred_element_type=jnp.float32)
    intermediate_signal_values = intermediate_signal.astype(jnp.float32)
    rank_everything = jnp.einsum("xz,szu->xsu", intermediate_signal_values, lowdim_entry_matrices.astype(jnp.float32))
    rank_in = jnp.sum(rank_everything * choose[:, :, None], axis=1)
    scatter_across_shards = choose[:, :, None] * rank_in[:, None, :]
    adapter_contribution = jnp.einsum("nwp,wpt->nt", scatter_across_shards, lowdim_exit_matrices.astype(jnp.float32))
    customized_projection_result = (base_term + adapter_contribution).astype(jnp.bfloat16)
    exit_matrix_derivative = jnp.einsum("zwy,zf->wyf", scatter_across_shards, result_sensitivity.astype(jnp.float32))
    backward_everything = jnp.einsum("sh,vzh->svz", result_sensitivity.astype(jnp.float32), lowdim_exit_matrices.astype(jnp.float32))
    rank_grad = jnp.sum(backward_everything * choose[:, :, None], axis=1)
    scatter_derivative = choose[:, :, None] * rank_grad[:, None, :]
    entry_matrix_derivative = jnp.einsum("vg,vqh->qgh", intermediate_signal_values, scatter_derivative)
    return customized_projection_result, entry_matrix_derivative, exit_matrix_derivative


def reference(intermediate_signal, frozen_down_weight, lowdim_entry_matrices, lowdim_exit_matrices, result_sensitivity, token_client_choice, matrix_bank_position, shard_active_entries):
    def batched_by_client(pieces):
        return single_group(pieces[0], frozen_down_weight, pieces[1], pieces[2], pieces[3], pieces[4], pieces[5], pieces[6])

    customized_projection_result, entry_matrix_derivative, exit_matrix_derivative = lax.map(batched_by_client, (intermediate_signal, lowdim_entry_matrices, lowdim_exit_matrices, result_sensitivity, token_client_choice, matrix_bank_position, shard_active_entries))
    return customized_projection_result, entry_matrix_derivative, exit_matrix_derivative
```

```python
import jax
import jax.numpy as jnp
from jax import lax
from jax.experimental import pallas as pl
from jax.experimental.pallas import tpu as pltpu
from jax.sharding import PartitionSpec as P

F32 = jnp.float32
BF16 = jnp.bfloat16
MESH = pl.DeviceIdType.MESH
SIDE = 4
RING = 8
CORES = 2
UP, DOWN = 3, 4
ORDER = [
    (0, 0), (1, 0), (3, 0), (0, 1),
    (0, 3), (1, 1), (3, 1), (1, 3),
    (3, 3), (2, 0), (0, 2), (1, 2),
    (2, 1), (2, 3), (3, 2), (2, 2),
]
GROUPS = 4
LANES = 128


def route(user_ids, slot_table, counts, n_src, cap):
    adapters = slot_table.shape[0]
    rows = user_ids.shape[0]
    tok = rows // n_src
    ids = jnp.arange(adapters, dtype=jnp.int32)
    storage = jnp.sum(jnp.where(user_ids[:, None] == ids[None, :], slot_table[None, :], 0), axis=1)
    place = jnp.arange(tok, dtype=jnp.int32)
    live = place[None, :] < counts[:, None]
    owner = jnp.where(live, storage.reshape(n_src, tok), -1)
    earlier = (owner[:, :, None] == owner[:, None, :]) & (place[None, None, :] < place[None, :, None])
    rank = jnp.sum(earlier.astype(jnp.int32), axis=2)
    slot = jnp.where(live, owner * cap + rank, -1)
    return owner, rank, slot


def halved(part, offset):
    dx, dy = offset
    first, last = (dx, dy) if part == 0 else (dy, dx)
    return last == 2 or (last == 0 and first == 2)


def exchange(
    x_ref, w_ref, b_ref, ranks_ref, sens_ref, put_ref,
    out_ref, exit_ref, grads_ref,
    x_sib, w_all, b_sib, b_all, y_all, rank_in, rank_own, rank_sib, rank_rows, sens_in, grad_out, grad_in,
    part_out, part_in, last_out, last_in, grad_sum,
    ag_send, ag_recv, rs_send, rs_recv, pair_send, pair_recv, all_send, all_recv,
):
    n = RING * CORES
    dp = lax.axis_index("dp")
    mp = lax.axis_index("mp")
    z, c = dp // CORES, dp % CORES
    my_y, my_x = mp // SIDE, mp % SIDE
    sib = dp + 1 - 2 * c
    depth = w_ref.shape[0]
    half = depth // 2
    rows = x_ref.shape[0]
    chip_rows = rows // RING
    own_rows = chip_rows // CORES
    wide = LANES * (len(ORDER) // GROUPS)
    features = b_ref.shape[1]
    width = b_ref.shape[0]

    def at_x(sign):
        return my_y * SIDE + (my_x + SIDE + sign) % SIDE

    def at_y(sign):
        return ((my_y + SIDE + sign) % SIDE) * SIDE + my_x

    barrier = pltpu.get_barrier_semaphore()
    for k in range(1, n):
        pl.semaphore_signal(barrier, inc=1, device_id={"dp": (dp + k) % n}, device_id_type=MESH)
    for to in (at_x(1), at_x(-1), at_y(1), at_y(-1)):
        pl.semaphore_signal(barrier, inc=1, device_id={"mp": to}, device_id_type=MESH)
    pl.semaphore_wait(barrier, n - 1 + 4)

    sent = []

    def send(src, dst, send_sem, recv_sem, to):
        copy = pltpu.make_async_remote_copy(
            src_ref=src, dst_ref=dst, send_sem=send_sem, recv_sem=recv_sem, device_id=to, device_id_type=MESH
        )
        copy.start()
        sent.append(copy)

    def arrived(dst, sem):
        pltpu.make_async_copy(dst, dst, sem).wait()

    names = {}

    def sem_of(part, offset, piece):
        return names.setdefault((part, offset, piece), len(names))

    def place(part, offset, piece=None):
        spot = ORDER.index(offset)
        cols = pl.ds(LANES * (spot % GROUPS), LANES)
        if piece is None:
            return w_all.at[part, spot // GROUPS, :, cols]
        return w_all.at[part, spot // GROUPS, pl.ds(half * piece, half), cols]

    def pass_on(axis, sign, part, offset, piece=None, src=None):
        dx, dy = offset
        seen = ((dx - sign) % SIDE, dy) if axis == "x" else (dx, (dy - sign) % SIDE)
        to = at_x(sign) if axis == "x" else at_y(sign)
        if src is None:
            src = place(part, offset, piece)
        num = sem_of(part, seen, piece)
        send(src, place(part, seen, piece), ag_send.at[num], ag_recv.at[num], {"mp": to})

    def got(part, offset):
        for piece in (0, 1) if halved(part, offset) else (None,):
            arrived(place(part, offset, piece), ag_recv.at[sem_of(part, offset, piece)])

    def both(axis, part, offset, src=None):
        for sign in (1, -1):
            pass_on(axis, sign, part, offset, None, src)

    def relay(axis, part, offset):
        away = offset[0] if axis == "x" else offset[1]
        if away == 1:
            pass_on(axis, -1, part, offset, 0)
        else:
            pass_on(axis, 1, part, offset, 1)

    own_cols = w_ref.at[:, pl.ds(pl.multiple_of(LANES * c, LANES), LANES)]
    sib_cols = w_ref.at[:, pl.ds(pl.multiple_of(LANES * (1 - c), LANES), LANES)]
    send(sib_cols, place(1, (0, 0)), pair_send.at[0], pair_recv.at[0], {"dp": sib})
    both("x", 0, (0, 0), own_cols)
    both("y", 0, (0, 0), own_cols)

    def to_all(sem, src_of, dst):
        def body(k, _):
            to = (dp + k) % n
            pltpu.make_async_remote_copy(
                src_ref=src_of(to), dst_ref=dst.at[dp], send_sem=all_send.at[sem], recv_sem=all_recv.at[sem],
                device_id={"dp": to}, device_id_type=MESH,
            ).start()
            return 0
        lax.fori_loop(1, n, body, 0)

    def all_done(sem, dst, src):
        arrived(dst.at[pl.ds(0, n - 1)], all_recv.at[sem])

    to_all(0, lambda to: ranks_ref.at[to], rank_in)
    send(x_ref, x_sib, pair_send.at[1], pair_recv.at[1], {"dp": sib})
    send(b_ref, b_sib, pair_send.at[2], pair_recv.at[2], {"dp": sib})
    to_all(1, lambda to: sens_ref.at[to], sens_in)

    w_all[0, 0, :, 0:LANES] = own_cols[...]
    rank_in[dp] = ranks_ref[dp]
    sens_in[dp] = sens_ref[dp]
    arrived(place(1, (0, 0)), pair_recv.at[0])
    both("y", 1, (0, 0))
    both("x", 1, (0, 0))

    for d in ((1, 0), (3, 0)):
        got(0, d)
        both("y", 0, d)
        relay("x", 0, d)
        e = (d[1], d[0])
        got(1, e)
        both("x", 1, e)
        relay("y", 1, e)

    all_done(0, rank_in, ranks_ref)
    total = rank_in[0].astype(F32)
    for k in range(1, n):
        total = total + rank_in[k].astype(F32)
    rank_own[...] = total
    send(rank_own, rank_sib, pair_send.at[3], pair_recv.at[3], {"dp": sib})
    arrived(b_sib, pair_recv.at[2])
    for g in range(GROUPS):
        for j in range(GROUPS):
            dx, dy = ORDER[g * GROUPS + j]
            m = ((my_y + dy) % SIDE) * SIDE + (my_x + dx) % SIDE
            col = pl.ds(pl.multiple_of(m * CORES * LANES + c * LANES, LANES), LANES)
            b_all[g, 0:width, j * LANES : (j + 1) * LANES] = b_ref[:, col]
            b_all[g, width : 2 * width, j * LANES : (j + 1) * LANES] = b_sib[:, col]
    arrived(rank_sib, pair_recv.at[3])
    lane = lax.broadcasted_iota(jnp.int32, rank_own.shape, 1)
    mine, theirs = rank_own[...], rank_sib[...]
    low = jnp.concatenate(
        [jnp.where(lane < width, mine, 0.0), jnp.where(lane < width, 0.0, pltpu.roll(theirs, width, 1))], axis=0
    ).astype(BF16)
    high = jnp.concatenate(
        [jnp.where(lane < width, pltpu.roll(mine, width, 1), 0.0), jnp.where(lane < width, 0.0, theirs)], axis=0
    ).astype(BF16)
    mid = rows // 2
    rank_rows[0:mid] = jnp.dot(put_ref[0:mid], low, preferred_element_type=F32).astype(BF16)
    rank_rows[mid:rows] = jnp.dot(put_ref[mid:rows], high, preferred_element_type=F32).astype(BF16)

    for d in ((1, 0), (3, 0)):
        e = (d[1], d[0])
        got(1, d)
        relay("x", 1, d)
        got(0, e)
        relay("y", 0, e)
    arrived(x_sib, pair_recv.at[1])

    def product(g):
        tile = rows // 4

        @pl.loop(0, 4)
        def _(i):
            at = pl.ds(pl.multiple_of(i * tile, tile), tile)
            y_all[g, at] = (
                jnp.dot(x_ref[at], w_all[0, g], preferred_element_type=F32)
                + jnp.dot(x_sib[at], w_all[1, g], preferred_element_type=F32)
                + jnp.dot(rank_rows[at], b_all[g], preferred_element_type=F32)
            )

    def sem_rs(g, way, step):
        return g * (UP + DOWN) + (step - 1 if way > 0 else UP + step - 1)

    def hop(g, step):
        for way, length in ((-1, DOWN), (1, UP)):
            if step > length:
                continue
            dest = (z + RING + way * (length + 1 - step)) % RING
            value = y_all[g, pl.ds(pl.multiple_of(dest * chip_rows, chip_rows), chip_rows)]
            if step > 1:
                before = sem_rs(g, way, step - 1)
                arrived(part_in.at[before], rs_recv.at[before])
                value = value + part_in[before].astype(F32)
            num = sem_rs(g, way, step)
            part_out[num] = value.astype(BF16)
            to = ((z + RING + way) % RING) * CORES + c
            send(part_out.at[num], part_in.at[num], rs_send.at[num], rs_recv.at[num], {"dp": to})

    def store(value, g, core):
        for j in range(GROUPS):
            dx, dy = ORDER[g * GROUPS + j]
            m = ((my_y + dy) % SIDE) * SIDE + (my_x + dx) % SIDE
            col = pl.ds(pl.multiple_of(m * CORES * LANES + core * LANES, LANES), LANES)
            out_ref[:, col] = value[:, j * LANES : (j + 1) * LANES]

    def finish(g):
        up, down = sem_rs(g, 1, UP), sem_rs(g, -1, DOWN)
        arrived(part_in.at[up], rs_recv.at[up])
        arrived(part_in.at[down], rs_recv.at[down])

        def rows_of(core):
            part = pl.ds(pl.multiple_of(core * own_rows, own_rows), own_rows)
            base = y_all[g, pl.ds(pl.multiple_of(z * chip_rows + core * own_rows, own_rows), own_rows)]
            return (base + part_in[up, part].astype(F32) + part_in[down, part].astype(F32)).astype(BF16)

        last_out[g] = rows_of(1 - c)
        send(last_out.at[g], last_in.at[g], pair_send.at[4 + g], pair_recv.at[4 + g], {"dp": sib})
        store(rows_of(c), g, c)

    def close(g):
        arrived(last_in.at[g], pair_recv.at[4 + g])
        store(last_in[g], g, 1 - c)

    product(0)
    hop(0, 1)
    for d in ((1, 1), (3, 1)):
        got(1, d)
        relay("x", 1, d)
        e = (d[1], d[0])
        got(0, e)
        relay("y", 0, e)
    for d in ((1, 3), (3, 3)):
        got(1, d)
        relay("x", 1, d)
        e = (d[1], d[0])
        got(0, e)
        relay("y", 0, e)
    got(0, (2, 0))
    both("y", 0, (2, 0))
    got(1, (0, 2))
    both("x", 1, (0, 2))
    product(1)
    hop(1, 1)
    hop(0, 2)

    all_done(1, sens_in, sens_ref)
    mine = rank_own[...]
    ranks = jnp.concatenate([mine[:, 0:width], mine[:, width : 2 * width]], axis=0).astype(BF16)
    grad_sum[...] = jnp.zeros_like(grad_sum)

    @pl.loop(0, features // wide)
    def _(i):
        at = pl.ds(pl.multiple_of(i * wide, wide), wide)
        block = sens_in[:, :, at].astype(F32).reshape(ranks.shape[0], wide).astype(BF16)
        exit_ref[:, at] = lax.dot_general(ranks, block, (((0,), (0,)), ((), ())), preferred_element_type=F32)
        grad_sum[...] += lax.dot_general(block, b_ref[:, at], (((1,), (1,)), ((), ())), preferred_element_type=F32)

    grad = grad_sum[...]
    grad_out[...] = jnp.concatenate([grad[0 : grad.shape[0] // 2], grad[grad.shape[0] // 2 :]], axis=1).astype(BF16)
    to_all(2, lambda to: grad_out, grad_in)
    grad_in[dp] = grad_out[...]

    hop(1, 2)
    hop(0, 3)
    for d in ((1, 2), (3, 2)):
        got(1, d)
        relay("x", 1, d)
        e = (d[1], d[0])
        got(0, e)
        relay("y", 0, e)
    hop(1, 3)
    hop(0, 4)
    for part in (0, 1):
        for d in ((2, 0), (0, 2), (1, 2)):
            if (part, d) not in ((0, (2, 0)), (1, (0, 2)), (1, (1, 2))):
                got(part, d)
    product(2)
    hop(2, 1)
    hop(1, 4)
    finish(0)
    for part in (0, 1):
        for d in ((2, 1), (2, 3), (3, 2), (2, 2)):
            if (part, d) not in ((0, (2, 1)), (0, (2, 3)), (1, (3, 2))):
                got(part, d)
    hop(2, 2)
    product(3)
    hop(3, 1)
    finish(1)
    hop(2, 3)
    hop(3, 2)
    close(0)
    close(1)
    all_done(2, grad_in, grad_out)
    grads_ref[...] = grad_in[...]
    hop(2, 4)
    hop(3, 3)
    finish(2)
    hop(3, 4)
    finish(3)
    close(2)
    close(3)

    for copy in sent:
        copy.wait_send()
    for k, src in enumerate((rank_in, sens_in, grad_in)):
        arrived(src.at[pl.ds(0, n - 1)], all_send.at[k])


def on_device(x, w, e, b, sens, user_ids, slot_table, counts):
    me = lax.axis_index("dp")
    n = lax.axis_size("dp")
    x, e, b, sens = x[0], e[0], b[0, 0], sens[0]
    rows, depth = x.shape
    tok = rows // n
    cap = tok // 8
    adapters, _, width = e.shape
    features = b.shape[1]
    slots = n * cap
    owner, rank, slot = route(user_ids[0], slot_table[0], counts[0], n, cap)
    pick = (slot[:, None, :] == jnp.arange(slots, dtype=jnp.int32)[None, :, None]).astype(BF16)
    my_pick = lax.dynamic_index_in_dim(pick, me, 0, keepdims=False)
    send_sens = jnp.dot(my_pick, sens, preferred_element_type=F32).astype(BF16).reshape(n, cap, features)
    choose = owner.reshape(rows)[:, None] == jnp.arange(adapters, dtype=jnp.int32)[None, :]
    every = jnp.einsum("xz,szu->xsu", x, e, preferred_element_type=F32)
    part = jnp.sum(every * choose.astype(F32)[:, :, None], axis=1).astype(BF16)
    send_rank = jnp.einsum("sqr,srf->sqf", pick, part.reshape(n, tok, width), preferred_element_type=F32)
    send_rank = send_rank.astype(BF16).reshape(2, n // 2, n, cap, width).transpose(2, 1, 3, 0, 4)
    send_rank = send_rank.reshape(n, slots // 2, 2 * width)
    spot = (jnp.arange(n, dtype=jnp.int32)[:, None] % (n // 2) * cap + rank).reshape(rows)
    column = jnp.arange(slots, dtype=jnp.int32)
    aim = jnp.where(column < slots // 2, me, me + 1 - 2 * (me % 2))
    put = ((owner.reshape(rows)[:, None] == aim[None, :]) & (spot[:, None] == column[None, :] % (slots // 2))).astype(BF16)

    vmem = pl.BlockSpec(memory_space=pltpu.VMEM)
    wide = features // CORES // GROUPS
    hops = GROUPS * (UP + DOWN)
    chip_rows = rows // RING
    out, exit_grad, grads = pl.pallas_call(
        exchange,
        out_shape=(
            jax.ShapeDtypeStruct((tok, features), BF16),
            jax.ShapeDtypeStruct((width, features), F32),
            jax.ShapeDtypeStruct((n, slots // 2, 2 * width), BF16),
        ),
        in_specs=[vmem] * 6,
        out_specs=(vmem,) * 3,
        scratch_shapes=[
            pltpu.VMEM((rows, depth), BF16),
            pltpu.VMEM((2, GROUPS, depth, wide), BF16),
            pltpu.VMEM((width, features), BF16),
            pltpu.VMEM((GROUPS, 2 * width, wide), BF16),
            pltpu.VMEM((GROUPS, rows, wide), F32),
            pltpu.VMEM((n, slots // 2, 2 * width), BF16),
            pltpu.VMEM((slots // 2, 2 * width), F32),
            pltpu.VMEM((slots // 2, 2 * width), F32),
            pltpu.VMEM((rows, 2 * width), BF16),
            pltpu.VMEM((n, cap, features), BF16),
            pltpu.VMEM((slots // 2, 2 * width), BF16),
            pltpu.VMEM((n, slots // 2, 2 * width), BF16),
            pltpu.VMEM((hops, chip_rows, wide), BF16),
            pltpu.VMEM((hops, chip_rows, wide), BF16),
            pltpu.VMEM((GROUPS, tok, wide), BF16),
            pltpu.VMEM((GROUPS, tok, wide), BF16),
            pltpu.VMEM((slots, width), F32),
            pltpu.SemaphoreType.DMA((40,)),
            pltpu.SemaphoreType.DMA((40,)),
            pltpu.SemaphoreType.DMA((hops,)),
            pltpu.SemaphoreType.DMA((hops,)),
            pltpu.SemaphoreType.DMA((8,)),
            pltpu.SemaphoreType.DMA((8,)),
            pltpu.SemaphoreType.DMA((3,)),
            pltpu.SemaphoreType.DMA((3,)),
        ],
        compiler_params=pltpu.CompilerParams(
            collective_id=0, has_side_effects=True, vmem_limit_bytes=60 * 1024 * 1024
        ),
    )(x, w, b, send_rank, send_sens, put)

    grads = grads.reshape(n, n // 2, cap, 2, width).transpose(3, 1, 0, 2, 4).reshape(n, slots, width)
    grad_rows = jnp.einsum("sqr,sqf->srf", pick, grads, preferred_element_type=F32)
    grad_rows = grad_rows.reshape(rows, width).astype(BF16)
    entry_grad = jnp.einsum(
        "vg,vqh->qgh", x, choose.astype(BF16)[:, :, None] * grad_rows[:, None, :], preferred_element_type=F32
    )
    return out[None], entry_grad[None], exit_grad[None, None]


def solution(mesh):
    in_specs = (
        P("mp", None, "dp"),
        P("dp", "mp"),
        P("mp", None, "dp", None),
        P("mp", "dp", None, None),
        P("mp", "dp", None),
        P("mp", None),
        P("mp", None),
        P("mp", None),
    )
    out_specs = (P("mp", "dp", None), P("mp", None, "dp", None), P("mp", "dp", None, None))
    return jax.shard_map(on_device, mesh=mesh, in_specs=in_specs, out_specs=out_specs, check_vma=False)
```

```python
import jax
import jax.numpy as jnp
from jax import lax
from jax.experimental import pallas as pl
from jax.experimental.pallas import tpu as pltpu
from jax.sharding import PartitionSpec as P

F32 = jnp.float32
BF16 = jnp.bfloat16
MESH = pl.DeviceIdType.MESH
SIDE = 4
RING = 8
CORES = 2
UP = (3, 4, 3, 4)
DOWN = (4, 3, 4, 3)
ORDER = [
    (0, 0), (1, 0), (3, 0), (0, 1),
    (0, 3), (1, 1), (3, 1), (1, 3),
    (3, 3), (2, 0), (0, 2), (1, 2),
    (2, 1), (2, 3), (3, 2), (2, 2),
]
GROUPS = 4
LANES = 128


def halved(part, offset):
    dx, dy = offset
    first, last = (dx, dy) if part == 0 else (dy, dx)
    return last == 2 or (last == 0 and first == 2)


def exchange(
    x_in, w_in, b_in, e_in, cotangent, users_ref, table_ref, counts_ref,
    out_ref, exit_ref, entry_ref,
    x_ref, w_ref, b_ref, e_ref, sens_ref, owner_ref, slot_ref, column_ref, ranks_out, sens_out,
    x_sib, w_all, b_sib, b_all, y_all, rank_in, rank_own, rank_sib, rank_rows, sens_in, grad_out, grad_in, grad_rows,
    part_out, part_in, last_out, last_in, grad_sum,
    ag_send, ag_recv, rs_send, rs_recv, pair_send, pair_recv, all_send, all_recv, load,
):
    n = RING * CORES
    dp = lax.axis_index("dp")
    mp = lax.axis_index("mp")
    z, c = dp // CORES, dp % CORES
    my_y, my_x = mp // SIDE, mp % SIDE
    sib = dp + 1 - 2 * c
    depth = w_ref.shape[0]
    half = depth // 2
    rows = x_ref.shape[0]
    chip_rows = rows // RING
    own_rows = chip_rows // CORES
    wide = LANES * (len(ORDER) // GROUPS)
    features = b_ref.shape[1]
    width = b_ref.shape[0]

    def at_x(sign):
        return my_y * SIDE + (my_x + SIDE + sign) % SIDE

    def at_y(sign):
        return ((my_y + SIDE + sign) % SIDE) * SIDE + my_x

    loads = [
        pltpu.make_async_copy(src, dst, load.at[k])
        for k, (src, dst) in enumerate(
            ((cotangent, sens_ref), (w_in, w_ref), (x_in, x_ref), (b_in, b_ref), (e_in, e_ref))
        )
    ]
    for copy in loads:
        copy.start()

    barrier = pltpu.get_barrier_semaphore()
    for k in range(1, n):
        pl.semaphore_signal(barrier, inc=1, device_id={"dp": (dp + k) % n}, device_id_type=MESH)
    for to in (at_x(1), at_x(-1), at_y(1), at_y(-1)):
        pl.semaphore_signal(barrier, inc=1, device_id={"mp": to}, device_id_type=MESH)

    adapters = n
    seg = rows // n
    cap = seg // 8
    blocks = rows // LANES
    users = users_ref[...]
    line = lax.broadcasted_iota(jnp.int32, users.shape, 0)
    lane = lax.broadcasted_iota(jnp.int32, users.shape, 1)
    upper = lane >= seg
    storage = jnp.zeros_like(users)
    limit = jnp.zeros_like(users)
    for k in range(n):
        storage = jnp.where(users == k, table_ref[k], storage)
        limit = jnp.where((line == k // CORES) & (upper == bool(k % CORES)), counts_ref[k], limit)
    owner = jnp.where(jnp.where(upper, lane - seg, lane) < limit, storage, -1)
    ids = lax.broadcasted_iota(jnp.int32, (adapters, LANES), 0)
    hot = jnp.concatenate([jnp.where(owner[k : k + 1] == ids, 1.0, 0.0) for k in range(blocks)], axis=0)
    r0 = lax.broadcasted_iota(jnp.int32, (LANES, LANES), 0)
    r1 = lax.broadcasted_iota(jnp.int32, (LANES, LANES), 1)
    before_me = jnp.where((r0 < r1) & ((r0 >= seg) == (r1 >= seg)), 1.0, 0.0).astype(BF16)
    count = jnp.dot(hot.astype(BF16), before_me, preferred_element_type=F32)
    order = jnp.sum((hot * count).reshape(blocks, adapters, LANES), axis=1)
    slot = jnp.where(owner < 0, -1.0, owner.astype(F32) * cap + order)
    spot = order + (line * cap + jnp.where(upper, seg, 0)).astype(F32)
    column = jnp.where(owner == dp, spot, jnp.where(owner == sib, spot + LANES, -1.0))
    owner_ref[...] = owner
    slot_ref[...] = slot
    column_ref[...] = column
    slot_ids = lax.broadcasted_iota(jnp.int32, (LANES, LANES), 0).astype(F32)
    in_upper = r1 >= seg

    def pick(k):
        return jnp.where(slot_ref[pl.ds(k, 1), :] == slot_ids, 1.0, 0.0).astype(BF16)

    loads[0].wait()
    one_hot = jnp.where((slot_ref[pl.ds(z, 1), :] == slot_ids) & (in_upper == (c == 1)), 1.0, 0.0).astype(BF16)

    @pl.loop(0, features // wide)
    def _(i):
        at = pl.ds(pl.multiple_of(i * wide, wide), wide)
        block = sens_ref[:, at]
        chosen = jnp.dot(one_hot, jnp.concatenate([block, block], axis=0), preferred_element_type=F32)
        sens_out[:, :, at] = chosen.reshape(n, cap, wide).astype(BF16)

    for copy in loads[1:4]:
        copy.wait()
    pl.semaphore_wait(barrier, n - 1 + 4)

    sent = []

    def send(src, dst, send_sem, recv_sem, to):
        copy = pltpu.make_async_remote_copy(
            src_ref=src, dst_ref=dst, send_sem=send_sem, recv_sem=recv_sem, device_id=to, device_id_type=MESH
        )
        copy.start()
        sent.append(copy)

    def arrived(dst, sem):
        pltpu.make_async_copy(dst, dst, sem).wait()

    names = {}

    def sem_of(part, offset, piece):
        return names.setdefault((part, offset, piece), len(names))

    def place(part, offset, piece=None):
        spot = ORDER.index(offset)
        cols = pl.ds(LANES * (spot % GROUPS), LANES)
        if piece is None:
            return w_all.at[part, spot // GROUPS, :, cols]
        return w_all.at[part, spot // GROUPS, pl.ds(half * piece, half), cols]

    def pass_on(axis, sign, part, offset, piece=None, src=None):
        dx, dy = offset
        seen = ((dx - sign) % SIDE, dy) if axis == "x" else (dx, (dy - sign) % SIDE)
        to = at_x(sign) if axis == "x" else at_y(sign)
        if src is None:
            src = place(part, offset, piece)
        num = sem_of(part, seen, piece)
        send(src, place(part, seen, piece), ag_send.at[num], ag_recv.at[num], {"mp": to})

    def got(part, offset):
        for piece in (0, 1) if halved(part, offset) else (None,):
            arrived(place(part, offset, piece), ag_recv.at[sem_of(part, offset, piece)])

    def both(axis, part, offset, src=None):
        for sign in (1, -1):
            pass_on(axis, sign, part, offset, None, src)

    def relay(axis, part, offset):
        away = offset[0] if axis == "x" else offset[1]
        if away == 1:
            pass_on(axis, -1, part, offset, 0)
        else:
            pass_on(axis, 1, part, offset, 1)

    own_cols = w_ref.at[:, pl.ds(pl.multiple_of(LANES * c, LANES), LANES)]
    sib_cols = w_ref.at[:, pl.ds(pl.multiple_of(LANES * (1 - c), LANES), LANES)]
    send(sib_cols, place(1, (0, 0)), pair_send.at[0], pair_recv.at[0], {"dp": sib})
    both("x", 0, (0, 0), own_cols)
    both("y", 0, (0, 0), own_cols)

    def to_all(sem, src_of, dst, spans):
        def body(k, _):
            to = (dp + k) % n
            pltpu.make_async_remote_copy(
                src_ref=src_of(to), dst_ref=dst.at[dp], send_sem=all_send.at[sem], recv_sem=all_recv.at[sem],
                device_id={"dp": to}, device_id_type=MESH,
            ).start()
            return 0
        for first, last in spans:
            lax.fori_loop(first, last, body, 0)

    def all_done(sem, dst):
        arrived(dst.at[pl.ds(0, n - 1)], all_recv.at[sem])

    to_all(1, lambda to: sens_out.at[to], sens_in, ((5, 7), (10, 12)))
    send(x_ref, x_sib, pair_send.at[1], pair_recv.at[1], {"dp": sib})
    send(b_ref, b_sib, pair_send.at[2], pair_recv.at[2], {"dp": sib})
    w_all[0, 0, :, 0:LANES] = own_cols[...]
    sens_in[dp] = sens_out[dp]
    arrived(place(1, (0, 0)), pair_recv.at[0])
    both("y", 1, (0, 0))
    both("x", 1, (0, 0))

    loads[4].wait()

    @pl.loop(0, blocks // 2)
    def _(i):
        tile = 2 * LANES
        every = lax.dot_general(
            e_ref[...], x_ref[pl.ds(pl.multiple_of(i * tile, tile), tile)], (((1,), (1,)), ((), ())),
            preferred_element_type=F32,
        )
        own = jnp.concatenate([owner_ref[pl.ds(2 * i, 1), :], owner_ref[pl.ds(2 * i + 1, 1), :]], axis=1)
        ranks = jnp.zeros((width, tile), F32)
        for k in range(adapters):
            ranks = ranks + jnp.where(own == k, every[k * width : (k + 1) * width], 0.0)
        for j in range(2):
            piece = ranks[:, j * LANES : (j + 1) * LANES]
            low = lax.broadcasted_iota(jnp.int32, piece.shape, 1) < seg
            spread = jnp.concatenate([jnp.where(low, piece, 0.0), jnp.where(low, 0.0, piece)], axis=0).astype(BF16)
            placed = lax.dot_general(pick(2 * i + j), spread, (((1,), (1,)), ((), ())), preferred_element_type=F32)
            ranks_out[:, pl.ds(2 * i + j, 1)] = placed.reshape(n, 1, cap, 2 * width).astype(BF16)

    to_all(0, lambda to: ranks_out.at[to], rank_in, ((1, n),))
    to_all(1, lambda to: sens_out.at[to], sens_in, ((1, 5), (7, 10), (12, n)))
    rank_in[dp] = ranks_out[dp]

    for d in ((1, 0), (3, 0)):
        got(0, d)
        both("y", 0, d)
        relay("x", 0, d)
    for e in ((0, 1), (0, 3)):
        got(1, e)
        both("x", 1, e)
        relay("y", 1, e)

    for d in ((1, 0), (3, 0)):
        e = (d[1], d[0])
        got(1, d)
        relay("x", 1, d)
        got(0, e)
        relay("y", 0, e)

    arrived(b_sib, pair_recv.at[2])
    for g in range(GROUPS):
        for j in range(GROUPS):
            dx, dy = ORDER[g * GROUPS + j]
            m = ((my_y + dy) % SIDE) * SIDE + (my_x + dx) % SIDE
            col = pl.ds(pl.multiple_of(m * CORES * LANES + c * LANES, LANES), LANES)
            b_all[g, 0:width, j * LANES : (j + 1) * LANES] = b_ref[:, col]
            b_all[g, width : 2 * width, j * LANES : (j + 1) * LANES] = b_sib[:, col]
    all_done(0, rank_in)
    total = rank_in[0].astype(F32)
    for k in range(1, n):
        total = total + rank_in[k].astype(F32)
    rank_own[...] = total.reshape(rank_own.shape)
    send(rank_own, rank_sib, pair_send.at[3], pair_recv.at[3], {"dp": sib})
    arrived(rank_sib, pair_recv.at[3])
    mine, theirs = rank_own[...], rank_sib[...]
    low = lax.broadcasted_iota(jnp.int32, mine.shape, 1) < width
    stack = jnp.concatenate(
        [
            jnp.where(low, mine, 0.0),
            jnp.where(low, pltpu.roll(mine, width, 1), 0.0),
            jnp.where(low, 0.0, pltpu.roll(theirs, width, 1)),
            jnp.where(low, 0.0, theirs),
        ],
        axis=0,
    ).astype(BF16)

    @pl.loop(0, blocks)
    def _(k):
        put = lax.broadcasted_iota(jnp.int32, (2 * LANES, LANES), 0).astype(F32) == column_ref[pl.ds(k, 1), :]
        put = jnp.where(put, 1.0, 0.0).astype(BF16)
        rank_rows[pl.ds(pl.multiple_of(k * LANES, LANES), LANES)] = lax.dot_general(
            put, stack, (((0,), (0,)), ((), ())), preferred_element_type=F32
        ).astype(BF16)

    arrived(x_sib, pair_recv.at[1])

    def product(g):
        tile = rows // 4

        @pl.loop(0, 4)
        def _(i):
            at = pl.ds(pl.multiple_of(i * tile, tile), tile)
            y_all[g, at] = (
                jnp.dot(x_ref[at], w_all[0, g], preferred_element_type=F32)
                + jnp.dot(x_sib[at], w_all[1, g], preferred_element_type=F32)
                + jnp.dot(rank_rows[at], b_all[g], preferred_element_type=F32)
            )

    def sem_rs(g, way, step):
        return g * (RING - 1) + (step - 1 if way > 0 else UP[g] + step - 1)

    def hop(g, step):
        for way, length in ((-1, DOWN[g]), (1, UP[g])):
            if step > length:
                continue
            dest = (z + RING + way * (length + 1 - step)) % RING
            value = y_all[g, pl.ds(pl.multiple_of(dest * chip_rows, chip_rows), chip_rows)]
            if step > 1:
                before = sem_rs(g, way, step - 1)
                arrived(part_in.at[before], rs_recv.at[before])
                value = value + part_in[before].astype(F32)
            num = sem_rs(g, way, step)
            part_out[num] = value.astype(BF16)
            to = ((z + RING + way) % RING) * CORES + c
            send(part_out.at[num], part_in.at[num], rs_send.at[num], rs_recv.at[num], {"dp": to})

    def store(value, g, core):
        for j in range(GROUPS):
            dx, dy = ORDER[g * GROUPS + j]
            m = ((my_y + dy) % SIDE) * SIDE + (my_x + dx) % SIDE
            col = pl.ds(pl.multiple_of(m * CORES * LANES + core * LANES, LANES), LANES)
            out_ref[:, col] = value[:, j * LANES : (j + 1) * LANES]

    def finish(g):
        up, down = sem_rs(g, 1, UP[g]), sem_rs(g, -1, DOWN[g])
        arrived(part_in.at[up], rs_recv.at[up])
        arrived(part_in.at[down], rs_recv.at[down])

        def rows_of(core):
            part = pl.ds(pl.multiple_of(core * own_rows, own_rows), own_rows)
            base = y_all[g, pl.ds(pl.multiple_of(z * chip_rows + core * own_rows, own_rows), own_rows)]
            return (base + part_in[up, part].astype(F32) + part_in[down, part].astype(F32)).astype(BF16)

        last_out[g] = rows_of(1 - c)
        send(last_out.at[g], last_in.at[g], pair_send.at[4 + g], pair_recv.at[4 + g], {"dp": sib})
        store(rows_of(c), g, c)

    def close(g):
        arrived(last_in.at[g], pair_recv.at[4 + g])
        store(last_in[g], g, 1 - c)

    def exit_and_rank_gradients():
        all_done(1, sens_in)
        mine = rank_own[...]
        halves = [mine[:, k * width : (k + 1) * width].reshape(blocks, 1, cap, width) for k in range(2)]
        ranks = jnp.concatenate(halves, axis=1).reshape(n * cap, width).astype(BF16)
        grad_sum[...] = jnp.zeros_like(grad_sum)

        @pl.loop(0, features // wide)
        def _(i):
            at = pl.ds(pl.multiple_of(i * wide, wide), wide)
            block = sens_in[:, :, at].astype(F32).reshape(n * cap, wide).astype(BF16)
            exit_ref[:, at] = lax.dot_general(ranks, block, (((0,), (0,)), ((), ())), preferred_element_type=F32)
            grad_sum[...] += lax.dot_general(
                block, b_ref[:, at], (((1,), (1,)), ((), ())), preferred_element_type=F32
            )

        grad = grad_sum[...].reshape(blocks, 2, cap, width)
        halves = [grad[:, k].reshape(blocks * cap, width) for k in range(2)]
        grad_out[...] = jnp.concatenate(halves, axis=1).reshape(blocks, cap, 2 * width).astype(BF16)
        to_all(2, lambda to: grad_out, grad_in, ((1, n),))
        grad_in[dp] = grad_out[...]

    def spread_gradients():
        all_done(2, grad_in)

        @pl.loop(0, blocks)
        def _(k):
            block = grad_in[:, pl.ds(k, 1)].astype(F32).reshape(n * cap, 2 * width).astype(BF16)
            both_halves = lax.dot_general(block, pick(k), (((0,), (0,)), ((), ())), preferred_element_type=F32)
            low = lax.broadcasted_iota(jnp.int32, (width, LANES), 1) < seg
            grads = jnp.where(low, both_halves[0:width], both_halves[width : 2 * width])
            own = owner_ref[pl.ds(k, 1), :]
            at = pl.ds(pl.multiple_of(k * LANES, LANES), LANES)
            for u in range(adapters):
                grad_rows[u * width : (u + 1) * width, at] = jnp.where(own == u, grads, 0.0).astype(BF16)

    def entry_gradient(i):
        tile = adapters * width // 4
        at = slice(i * tile, (i + 1) * tile)
        entry_ref[at] = jnp.dot(grad_rows[at], x_ref[...], preferred_element_type=F32)

    product(0)
    hop(0, 1)
    for d in ((1, 1), (3, 1), (1, 3), (3, 3)):
        got(1, d)
        relay("x", 1, d)
        e = (d[1], d[0])
        got(0, e)
        relay("y", 0, e)
    got(0, (2, 0))
    both("y", 0, (2, 0))
    got(1, (0, 2))
    both("x", 1, (0, 2))
    product(1)
    hop(1, 1)
    hop(0, 2)
    for d in ((1, 2), (3, 2)):
        got(1, d)
        relay("x", 1, d)
        e = (d[1], d[0])
        got(0, e)
        relay("y", 0, e)
    hop(0, 3)
    hop(1, 2)
    exit_and_rank_gradients()
    for part in (0, 1):
        for d in ((2, 0), (0, 2), (1, 2)):
            if (part, d) not in ((0, (2, 0)), (1, (0, 2)), (1, (1, 2))):
                got(part, d)
    product(2)
    hop(2, 1)
    hop(1, 3)
    hop(0, 4)
    for part in (0, 1):
        for d in ((2, 1), (2, 3), (3, 2), (2, 2)):
            if (part, d) not in ((0, (2, 1)), (0, (2, 3)), (1, (3, 2))):
                got(part, d)
    product(3)
    hop(3, 1)
    hop(2, 2)
    hop(1, 4)
    finish(0)
    spread_gradients()
    hop(3, 2)
    hop(2, 3)
    finish(1)
    entry_gradient(0)
    entry_gradient(1)
    hop(3, 3)
    hop(2, 4)
    entry_gradient(2)
    entry_gradient(3)
    hop(3, 4)
    close(0)
    close(1)
    finish(2)
    close(2)
    finish(3)
    close(3)

    for copy in sent:
        copy.wait_send()
    for k, src in enumerate((rank_in, sens_in, grad_in)):
        arrived(src.at[pl.ds(0, n - 1)], all_send.at[k])


def on_device(x, w, e, b, sens, user_ids, slot_table, counts):
    n = lax.axis_size("dp")
    x, e, b, sens = x[0], e[0], b[0, 0], sens[0]
    rows, depth = x.shape
    tok = rows // n
    cap = tok // 8
    adapters, _, width = e.shape
    features = b.shape[1]
    slots = n * cap
    blocks = rows // LANES
    wide = features // CORES // GROUPS
    hops = GROUPS * (RING - 1)
    chip_rows = rows // RING
    vmem = pl.BlockSpec(memory_space=pltpu.VMEM)
    smem = pl.BlockSpec(memory_space=pltpu.SMEM)
    out, exit_grad, entry_grad = pl.pallas_call(
        exchange,
        out_shape=(
            jax.ShapeDtypeStruct((tok, features), BF16),
            jax.ShapeDtypeStruct((width, features), F32),
            jax.ShapeDtypeStruct((adapters * width, depth), F32),
        ),
        in_specs=[pl.BlockSpec(memory_space=pl.ANY)] * 5 + [vmem] + [smem] * 2,
        out_specs=(vmem,) * 3,
        scratch_shapes=[
            pltpu.VMEM((rows, depth), BF16),
            pltpu.VMEM(w.shape, BF16),
            pltpu.VMEM((width, features), BF16),
            pltpu.VMEM((adapters * width, depth), BF16),
            pltpu.VMEM((tok, features), BF16),
            pltpu.VMEM((blocks, LANES), jnp.int32),
            pltpu.VMEM((blocks, LANES), F32),
            pltpu.VMEM((blocks, LANES), F32),
            pltpu.VMEM((n, blocks, cap, 2 * width), BF16),
            pltpu.VMEM((n, cap, features), BF16),
            pltpu.VMEM((rows, depth), BF16),
            pltpu.VMEM((2, GROUPS, depth, wide), BF16),
            pltpu.VMEM((width, features), BF16),
            pltpu.VMEM((GROUPS, 2 * width, wide), BF16),
            pltpu.VMEM((GROUPS, rows, wide), F32),
            pltpu.VMEM((n, blocks, cap, 2 * width), BF16),
            pltpu.VMEM((slots // 2, 2 * width), F32),
            pltpu.VMEM((slots // 2, 2 * width), F32),
            pltpu.VMEM((rows, 2 * width), BF16),
            pltpu.VMEM((n, cap, features), BF16),
            pltpu.VMEM((blocks, cap, 2 * width), BF16),
            pltpu.VMEM((n, blocks, cap, 2 * width), BF16),
            pltpu.VMEM((adapters * width, rows), BF16),
            pltpu.VMEM((hops, chip_rows, wide), BF16),
            pltpu.VMEM((hops, chip_rows, wide), BF16),
            pltpu.VMEM((GROUPS, tok, wide), BF16),
            pltpu.VMEM((GROUPS, tok, wide), BF16),
            pltpu.VMEM((slots, width), F32),
            pltpu.SemaphoreType.DMA((40,)),
            pltpu.SemaphoreType.DMA((40,)),
            pltpu.SemaphoreType.DMA((hops,)),
            pltpu.SemaphoreType.DMA((hops,)),
            pltpu.SemaphoreType.DMA((8,)),
            pltpu.SemaphoreType.DMA((8,)),
            pltpu.SemaphoreType.DMA((3,)),
            pltpu.SemaphoreType.DMA((3,)),
            pltpu.SemaphoreType.DMA((5,)),
        ],
        compiler_params=pltpu.CompilerParams(
            collective_id=0, has_side_effects=True, vmem_limit_bytes=62 * 1024 * 1024
        ),
    )(
        x,
        w,
        b,
        e.transpose(0, 2, 1).reshape(adapters * width, depth),
        sens,
        user_ids.reshape(blocks, LANES),
        slot_table[0],
        counts[0],
    )
    entry_grad = entry_grad.reshape(adapters, width, depth).transpose(0, 2, 1)
    return out[None], entry_grad[None], exit_grad[None, None]


def solution(mesh):
    in_specs = (
        P("mp", None, "dp"),
        P("dp", "mp"),
        P("mp", None, "dp", None),
        P("mp", "dp", None, None),
        P("mp", "dp", None),
        P("mp", None),
        P("mp", None),
        P("mp", None),
    )
    out_specs = (P("mp", "dp", None), P("mp", None, "dp", None), P("mp", "dp", None, None))
    return jax.shard_map(on_device, mesh=mesh, in_specs=in_specs, out_specs=out_specs, check_vma=False)
```

```python
import jax
import jax.numpy as jnp
from jax import lax
from jax.experimental import pallas as pl
from jax.experimental.pallas import tpu as pltpu
from jax.sharding import PartitionSpec as P

F32 = jnp.float32
BF16 = jnp.bfloat16
MESH = pl.DeviceIdType.MESH
SIDE = 4
RING = 8
CORES = 2
UP = (3, 4, 3, 4)
DOWN = (4, 3, 4, 3)
ORDER = [
    (0, 0), (1, 0), (3, 0), (0, 1),
    (0, 3), (1, 1), (3, 1), (1, 3),
    (3, 3), (2, 0), (0, 2), (1, 2),
    (2, 1), (2, 3), (3, 2), (2, 2),
]
GROUPS = 4
LANES = 128


def halved(part, offset):
    dx, dy = offset
    first, last = (dx, dy) if part == 0 else (dy, dx)
    return last == 2 or (last == 0 and first == 2)


def exchange(
    x_in, w_in, b_in, e_in, cotangent, users_ref, table_ref, counts_ref,
    out_ref, exit_ref, entry_ref,
    x_ref, w_ref, b_ref, e_ref, sens_ref, owner_ref, slot_ref, column_ref, ranks_out, sens_out,
    x_sib, w_all, b_sib, b_all, y_all, rank_pair, pair_sum, rank_in, rank_own, rank_sib, rank_rows, sens_in, grad_out, grad_in, grad_rows,
    part_out, part_in, near_out, near_in, last_in, grad_sum,
    ag_send, ag_recv, rs_send, rs_recv, pair_send, pair_recv, all_send, all_recv, load, last_send, last_recv,
):
    n = RING * CORES
    dp = lax.axis_index("dp")
    mp = lax.axis_index("mp")
    z, c = dp // CORES, dp % CORES
    my_y, my_x = mp // SIDE, mp % SIDE
    sib = dp + 1 - 2 * c
    depth = w_ref.shape[0]
    half = depth // 2
    rows = x_ref.shape[0]
    chip_rows = rows // RING
    own_rows = chip_rows // CORES
    wide = LANES * (len(ORDER) // GROUPS)
    features = b_ref.shape[1]
    width = b_ref.shape[0]

    def at_x(sign):
        return my_y * SIDE + (my_x + SIDE + sign) % SIDE

    def at_y(sign):
        return ((my_y + SIDE + sign) % SIDE) * SIDE + my_x

    loads = [
        pltpu.make_async_copy(src, dst, load.at[k])
        for k, (src, dst) in enumerate(
            ((cotangent, sens_ref), (w_in, w_ref), (x_in, x_ref), (b_in, b_ref), (e_in, e_ref))
        )
    ]
    for copy in loads:
        copy.start()

    barrier = pltpu.get_barrier_semaphore()
    for k in range(1, n):
        pl.semaphore_signal(barrier, inc=1, device_id={"dp": (dp + k) % n}, device_id_type=MESH)
    for to in (at_x(1), at_x(-1), at_y(1), at_y(-1)):
        pl.semaphore_signal(barrier, inc=1, device_id={"mp": to}, device_id_type=MESH)

    adapters = n
    seg = rows // n
    cap = seg // 8
    blocks = rows // LANES
    users = users_ref[...]
    line = lax.broadcasted_iota(jnp.int32, users.shape, 0)
    lane = lax.broadcasted_iota(jnp.int32, users.shape, 1)
    upper = lane >= seg
    storage = jnp.zeros_like(users)
    limit = jnp.zeros_like(users)
    for k in range(n):
        storage = jnp.where(users == k, table_ref[k], storage)
        limit = jnp.where((line == k // CORES) & (upper == bool(k % CORES)), counts_ref[k], limit)
    owner = jnp.where(jnp.where(upper, lane - seg, lane) < limit, storage, -1)
    ids = lax.broadcasted_iota(jnp.int32, (adapters, LANES), 0)
    hot = jnp.concatenate([jnp.where(owner[k : k + 1] == ids, 1.0, 0.0) for k in range(blocks)], axis=0)
    r0 = lax.broadcasted_iota(jnp.int32, (LANES, LANES), 0)
    r1 = lax.broadcasted_iota(jnp.int32, (LANES, LANES), 1)
    before_me = jnp.where((r0 < r1) & ((r0 >= seg) == (r1 >= seg)), 1.0, 0.0).astype(BF16)
    count = jnp.dot(hot.astype(BF16), before_me, preferred_element_type=F32)
    order = jnp.sum((hot * count).reshape(blocks, adapters, LANES), axis=1)
    slot = jnp.where(owner < 0, -1.0, owner.astype(F32) * cap + order)
    spot = order + (line * cap + jnp.where(upper, seg, 0)).astype(F32)
    column = jnp.where(owner == dp, spot, jnp.where(owner == sib, spot + LANES, -1.0))
    owner_ref[...] = owner
    slot_ref[...] = slot
    column_ref[...] = column
    slot_ids = lax.broadcasted_iota(jnp.int32, (LANES, LANES), 0).astype(F32)
    in_upper = r1 >= seg

    def pick(k):
        return jnp.where(slot_ref[pl.ds(k, 1), :] == slot_ids, 1.0, 0.0).astype(BF16)

    loads[0].wait()
    one_hot = jnp.where((slot_ref[pl.ds(z, 1), :] == slot_ids) & (in_upper == (c == 1)), 1.0, 0.0).astype(BF16)

    @pl.loop(0, features // wide)
    def _(i):
        at = pl.ds(pl.multiple_of(i * wide, wide), wide)
        block = sens_ref[:, at]
        chosen = jnp.dot(one_hot, jnp.concatenate([block, block], axis=0), preferred_element_type=F32)
        sens_out[:, :, at] = chosen.reshape(n, cap, wide).astype(BF16)

    for copy in loads[1:4]:
        copy.wait()
    pl.semaphore_wait(barrier, n - 1 + 4)

    sent = []

    def send(src, dst, send_sem, recv_sem, to):
        copy = pltpu.make_async_remote_copy(
            src_ref=src, dst_ref=dst, send_sem=send_sem, recv_sem=recv_sem, device_id=to, device_id_type=MESH
        )
        copy.start()
        sent.append(copy)

    def arrived(dst, sem):
        pltpu.make_async_copy(dst, dst, sem).wait()

    names = {}

    def sem_of(part, offset, piece):
        return names.setdefault((part, offset, piece), len(names))

    def place(part, offset, piece=None):
        spot = ORDER.index(offset)
        cols = pl.ds(LANES * (spot % GROUPS), LANES)
        if piece is None:
            return w_all.at[part, spot // GROUPS, :, cols]
        return w_all.at[part, spot // GROUPS, pl.ds(half * piece, half), cols]

    def pass_on(axis, sign, part, offset, piece=None, src=None):
        dx, dy = offset
        seen = ((dx - sign) % SIDE, dy) if axis == "x" else (dx, (dy - sign) % SIDE)
        to = at_x(sign) if axis == "x" else at_y(sign)
        if src is None:
            src = place(part, offset, piece)
        num = sem_of(part, seen, piece)
        send(src, place(part, seen, piece), ag_send.at[num], ag_recv.at[num], {"mp": to})

    def got(part, offset):
        for piece in (0, 1) if halved(part, offset) else (None,):
            arrived(place(part, offset, piece), ag_recv.at[sem_of(part, offset, piece)])

    def both(axis, part, offset, src=None):
        for sign in (1, -1):
            pass_on(axis, sign, part, offset, None, src)

    def relay(axis, part, offset):
        away = offset[0] if axis == "x" else offset[1]
        if away == 1:
            pass_on(axis, -1, part, offset, 0)
        else:
            pass_on(axis, 1, part, offset, 1)

    def to_all(sem, src_of, dst, spans):
        def body(k, _):
            to = (dp + k) % n
            pltpu.make_async_remote_copy(
                src_ref=src_of(to), dst_ref=dst.at[dp], send_sem=all_send.at[sem], recv_sem=all_recv.at[sem],
                device_id={"dp": to}, device_id_type=MESH,
            ).start()
            return 0
        for first, last in spans:
            lax.fori_loop(first, last, body, 0)

    def to_chips(sem, src_of, dst):
        def body(k, _):
            to = (z + k) % RING
            pltpu.make_async_remote_copy(
                src_ref=src_of(to), dst_ref=dst, send_sem=all_send.at[sem], recv_sem=all_recv.at[sem],
                device_id={"dp": to * CORES + c}, device_id_type=MESH,
            ).start()
            return 0
        lax.fori_loop(1, RING, body, 0)

    to_all(1, lambda to: sens_out.at[to], sens_in, ((5, 7), (10, 12)))

    own_cols = w_ref.at[:, pl.ds(pl.multiple_of(LANES * c, LANES), LANES)]
    sib_cols = w_ref.at[:, pl.ds(pl.multiple_of(LANES * (1 - c), LANES), LANES)]
    send(sib_cols, place(1, (0, 0)), pair_send.at[0], pair_recv.at[0], {"dp": sib})
    both("x", 0, (0, 0), own_cols)
    send(x_ref, x_sib, pair_send.at[1], pair_recv.at[1], {"dp": sib})
    send(b_ref, b_sib, pair_send.at[2], pair_recv.at[2], {"dp": sib})
    w_all[0, 0, :, 0:LANES] = own_cols[...]
    sens_in[dp] = sens_out[dp]
    arrived(place(1, (0, 0)), pair_recv.at[0])
    both("y", 1, (0, 0))
    both("y", 0, (0, 0), own_cols)
    both("x", 1, (0, 0))

    loads[4].wait()

    @pl.loop(0, blocks // 2)
    def _(i):
        tile = 2 * LANES
        every = lax.dot_general(
            e_ref[...], x_ref[pl.ds(pl.multiple_of(i * tile, tile), tile)], (((1,), (1,)), ((), ())),
            preferred_element_type=F32,
        )
        own = jnp.concatenate([owner_ref[pl.ds(2 * i, 1), :], owner_ref[pl.ds(2 * i + 1, 1), :]], axis=1)
        ranks = jnp.zeros((width, tile), F32)
        for k in range(adapters):
            ranks = ranks + jnp.where(own == k, every[k * width : (k + 1) * width], 0.0)
        for j in range(2):
            piece = ranks[:, j * LANES : (j + 1) * LANES]
            low = lax.broadcasted_iota(jnp.int32, piece.shape, 1) < seg
            spread = jnp.concatenate([jnp.where(low, piece, 0.0), jnp.where(low, 0.0, piece)], axis=0).astype(BF16)
            placed = lax.dot_general(pick(2 * i + j), spread, (((1,), (1,)), ((), ())), preferred_element_type=F32)
            placed = placed.reshape(RING, CORES, 1, cap, 2 * width).astype(BF16)
            for core in range(CORES):
                ranks_out[core, :, pl.ds(2 * i + j, 1)] = placed[:, core]

    send(ranks_out.at[1 - c], rank_pair, pair_send.at[8], pair_recv.at[8], {"dp": sib})
    arrived(rank_pair, pair_recv.at[8])
    pair_sum[...] = (ranks_out[c].astype(F32) + rank_pair[...].astype(F32)).astype(BF16)
    to_chips(0, lambda to: pair_sum.at[to], rank_in.at[z])
    to_all(1, lambda to: sens_out.at[to], sens_in, ((1, 5), (7, 10), (12, n)))
    rank_in[z] = pair_sum[z]

    for d in ((1, 0), (3, 0)):
        got(0, d)
        both("y", 0, d)
        relay("x", 0, d)
    for e in ((0, 1), (0, 3)):
        got(1, e)
        both("x", 1, e)
        relay("y", 1, e)

    for d in ((1, 0), (3, 0)):
        e = (d[1], d[0])
        got(1, d)
        relay("x", 1, d)
        got(0, e)
        relay("y", 0, e)

    arrived(b_sib, pair_recv.at[2])
    for g in range(GROUPS):
        for j in range(GROUPS):
            dx, dy = ORDER[g * GROUPS + j]
            m = ((my_y + dy) % SIDE) * SIDE + (my_x + dx) % SIDE
            col = pl.ds(pl.multiple_of(m * CORES * LANES + c * LANES, LANES), LANES)
            b_all[g, 0:width, j * LANES : (j + 1) * LANES] = b_ref[:, col]
            b_all[g, width : 2 * width, j * LANES : (j + 1) * LANES] = b_sib[:, col]
    arrived(rank_in.at[pl.ds(0, RING - 1)], all_recv.at[0])
    total = rank_in[0].astype(F32)
    for k in range(1, RING):
        total = total + rank_in[k].astype(F32)
    rank_own[...] = total.reshape(rank_own.shape)
    send(rank_own, rank_sib, pair_send.at[3], pair_recv.at[3], {"dp": sib})
    arrived(rank_sib, pair_recv.at[3])
    mine, theirs = rank_own[...], rank_sib[...]
    low = lax.broadcasted_iota(jnp.int32, mine.shape, 1) < width
    stack = jnp.concatenate(
        [
            jnp.where(low, mine, 0.0),
            jnp.where(low, pltpu.roll(mine, width, 1), 0.0),
            jnp.where(low, 0.0, pltpu.roll(theirs, width, 1)),
            jnp.where(low, 0.0, theirs),
        ],
        axis=0,
    ).astype(BF16)

    @pl.loop(0, blocks)
    def _(k):
        put = lax.broadcasted_iota(jnp.int32, (2 * LANES, LANES), 0).astype(F32) == column_ref[pl.ds(k, 1), :]
        put = jnp.where(put, 1.0, 0.0).astype(BF16)
        rank_rows[pl.ds(pl.multiple_of(k * LANES, LANES), LANES)] = lax.dot_general(
            put, stack, (((0,), (0,)), ((), ())), preferred_element_type=F32
        ).astype(BF16)

    arrived(x_sib, pair_recv.at[1])

    def product(g):
        tile = rows // 4

        @pl.loop(0, 4)
        def _(i):
            at = pl.ds(pl.multiple_of(i * tile, tile), tile)
            y_all[g, at] = (
                jnp.dot(x_ref[at], w_all[0, g], preferred_element_type=F32)
                + jnp.dot(x_sib[at], w_all[1, g], preferred_element_type=F32)
                + jnp.dot(rank_rows[at], b_all[g], preferred_element_type=F32)
            )

    def sem_rs(g, way, step):
        return g * (RING - 1) + (step - 1 if way > 0 else UP[g] + step - 1)

    def hop(g, step):
        for way, length in ((-1, DOWN[g]), (1, UP[g])):
            if step > length:
                continue
            dest = (z + RING + way * (length + 1 - step)) % RING
            value = y_all[g, pl.ds(pl.multiple_of(dest * chip_rows, chip_rows), chip_rows)]
            if step > 1:
                before = sem_rs(g, way, step - 1)
                arrived(part_in.at[before], rs_recv.at[before])
                value = value + part_in[before].astype(F32)
            num = sem_rs(g, way, step)
            part_out[num] = value.astype(BF16)
            to = ((z + RING + way) % RING) * CORES
            if step < length:
                send(part_out.at[num], part_in.at[num], rs_send.at[num], rs_recv.at[num], {"dp": to + c})
                continue
            side = (1 + way) // 2
            for core in range(CORES):
                piece = part_out.at[num, pl.ds(core * own_rows, own_rows)]
                out_sem = last_send.at[g * 4 + side * 2 + core]
                send(piece, last_in.at[g, side, c], out_sem, last_recv.at[g * 4 + side * 2 + c], {"dp": to + core})

    def store(value, g, core):
        for j in range(GROUPS):
            dx, dy = ORDER[g * GROUPS + j]
            m = ((my_y + dy) % SIDE) * SIDE + (my_x + dx) % SIDE
            col = pl.ds(pl.multiple_of(m * CORES * LANES + core * LANES, LANES), LANES)
            out_ref[:, col] = value[:, j * LANES : (j + 1) * LANES]

    def rows_of(g, core):
        return y_all[g, pl.ds(pl.multiple_of(z * chip_rows + core * own_rows, own_rows), own_rows)]

    def lend(g):
        near_out[g] = rows_of(g, 1 - c).astype(BF16)
        send(near_out.at[g], near_in.at[g], pair_send.at[4 + g], pair_recv.at[4 + g], {"dp": sib})

    def finish(g):
        arrived(near_in.at[g], pair_recv.at[4 + g])
        for side in range(2):
            for core in range(CORES):
                arrived(last_in.at[g, side, core], last_recv.at[g * 4 + side * 2 + core])
        value = rows_of(g, c) + last_in[g, 0, c].astype(F32) + last_in[g, 1, c].astype(F32)
        store(value.astype(BF16), g, c)
        value = near_in[g].astype(F32) + last_in[g, 0, 1 - c].astype(F32) + last_in[g, 1, 1 - c].astype(F32)
        store(value.astype(BF16), g, 1 - c)

    def drain(count):
        for copy in sent[:count]:
            copy.wait_send()
        del sent[:count]

    def exit_and_rank_gradients():
        arrived(sens_in.at[pl.ds(0, n - 1)], all_recv.at[1])
        mine = rank_own[...]
        halves = [mine[:, k * width : (k + 1) * width].reshape(blocks, 1, cap, width) for k in range(2)]
        ranks = jnp.concatenate(halves, axis=1).reshape(n * cap, width).astype(BF16)
        grad_sum[...] = jnp.zeros_like(grad_sum)

        @pl.loop(0, features // wide)
        def _(i):
            at = pl.ds(pl.multiple_of(i * wide, wide), wide)
            block = sens_in[:, :, at].astype(F32).reshape(n * cap, wide).astype(BF16)
            exit_ref[:, at] = lax.dot_general(ranks, block, (((0,), (0,)), ((), ())), preferred_element_type=F32)
            grad_sum[...] += lax.dot_general(
                block, b_ref[:, at], (((1,), (1,)), ((), ())), preferred_element_type=F32
            )

        grad = grad_sum[...].reshape(blocks, 2, cap, width)
        halves = [grad[:, k].reshape(blocks * cap, width) for k in range(2)]
        grad_out[...] = jnp.concatenate(halves, axis=1).reshape(blocks, cap, 2 * width).astype(BF16)
        to_chips(2, lambda to: grad_out, grad_in.at[c, z])
        grad_in[c, z] = grad_out[...]

    def swap_gradients():
        arrived(grad_in.at[0, pl.ds(0, RING - 1)], all_recv.at[2])
        send(grad_in.at[c], grad_in.at[c], pair_send.at[9], pair_recv.at[9], {"dp": sib})

    def spread_gradients():
        arrived(grad_in.at[0], pair_recv.at[9])

        @pl.loop(0, blocks)
        def _(k):
            block = jnp.concatenate([grad_in[core, :, pl.ds(k, 1)].astype(F32) for core in range(CORES)], axis=1)
            block = block.reshape(n * cap, 2 * width).astype(BF16)
            both_halves = lax.dot_general(block, pick(k), (((0,), (0,)), ((), ())), preferred_element_type=F32)
            low = lax.broadcasted_iota(jnp.int32, (width, LANES), 1) < seg
            grads = jnp.where(low, both_halves[0:width], both_halves[width : 2 * width])
            own = owner_ref[pl.ds(k, 1), :]
            at = pl.ds(pl.multiple_of(k * LANES, LANES), LANES)
            for u in range(adapters):
                grad_rows[u * width : (u + 1) * width, at] = jnp.where(own == u, grads, 0.0).astype(BF16)

    def entry_gradient(i):
        tile = adapters * width // 4
        at = slice(i * tile, (i + 1) * tile)
        entry_ref[at] = jnp.dot(grad_rows[at], x_ref[...], preferred_element_type=F32)

    product(0)
    hop(0, 1)
    for d in ((1, 1), (3, 1), (1, 3), (3, 3)):
        got(1, d)
        relay("x", 1, d)
        e = (d[1], d[0])
        got(0, e)
        relay("y", 0, e)
    got(0, (2, 0))
    both("y", 0, (2, 0))
    got(1, (0, 2))
    both("x", 1, (0, 2))
    product(1)
    hop(1, 1)
    hop(0, 2)
    lend(0)
    exit_and_rank_gradients()
    got(1, (1, 2))
    relay("x", 1, (1, 2))
    got(0, (2, 1))
    relay("y", 0, (2, 1))
    hop(0, 3)
    got(1, (3, 2))
    relay("x", 1, (3, 2))
    got(0, (2, 3))
    relay("y", 0, (2, 3))
    hop(1, 2)
    lend(1)
    for part in (0, 1):
        for d in ((2, 0), (0, 2), (1, 2)):
            if (part, d) not in ((0, (2, 0)), (1, (0, 2)), (1, (1, 2))):
                got(part, d)
    product(2)
    hop(2, 1)
    for part in (0, 1):
        for d in ((2, 1), (2, 3), (3, 2), (2, 2)):
            if (part, d) not in ((0, (2, 1)), (0, (2, 3)), (1, (3, 2))):
                got(part, d)
    product(3)
    hop(3, 1)
    hop(1, 3)
    hop(0, 4)
    issued = len(sent)
    lend(2)
    lend(3)
    swap_gradients()
    hop(2, 2)
    spread_gradients()
    hop(3, 2)
    hop(1, 4)
    finish(0)
    entry_gradient(0)
    hop(2, 3)
    entry_gradient(1)
    finish(1)
    hop(3, 3)
    entry_gradient(2)
    hop(2, 4)
    entry_gradient(3)
    drain(issued)
    hop(3, 4)
    finish(2)
    finish(3)

    for copy in sent:
        copy.wait_send()
    arrived(rank_in.at[pl.ds(0, RING - 1)], all_send.at[0])
    arrived(sens_in.at[pl.ds(0, n - 1)], all_send.at[1])
    arrived(rank_in.at[pl.ds(0, RING - 1)], all_send.at[2])


def on_device(x, w, e, b, sens, user_ids, slot_table, counts):
    n = lax.axis_size("dp")
    x, e, b, sens = x[0], e[0], b[0, 0], sens[0]
    rows, depth = x.shape
    tok = rows // n
    cap = tok // 8
    adapters, _, width = e.shape
    features = b.shape[1]
    slots = n * cap
    blocks = rows // LANES
    wide = features // CORES // GROUPS
    hops = GROUPS * (RING - 1)
    chip_rows = rows // RING
    vmem = pl.BlockSpec(memory_space=pltpu.VMEM)
    smem = pl.BlockSpec(memory_space=pltpu.SMEM)
    out, exit_grad, entry_grad = pl.pallas_call(
        exchange,
        out_shape=(
            pltpu.VMEM((tok, features), BF16),
            pltpu.VMEM((width, features), F32),
            pltpu.VMEM((adapters * width, depth), F32),
        ),
        in_specs=[pl.BlockSpec(memory_space=pl.ANY)] * 5 + [vmem] + [smem] * 2,
        out_specs=(vmem,) * 3,
        scratch_shapes=[
            pltpu.VMEM((rows, depth), BF16),
            pltpu.VMEM(w.shape, BF16),
            pltpu.VMEM((width, features), BF16),
            pltpu.VMEM((adapters * width, depth), BF16),
            pltpu.VMEM((tok, features), BF16),
            pltpu.VMEM((blocks, LANES), jnp.int32),
            pltpu.VMEM((blocks, LANES), F32),
            pltpu.VMEM((blocks, LANES), F32),
            pltpu.VMEM((CORES, RING, blocks, cap, 2 * width), BF16),
            pltpu.VMEM((n, cap, features), BF16),
            pltpu.VMEM((rows, depth), BF16),
            pltpu.VMEM((2, GROUPS, depth, wide), BF16),
            pltpu.VMEM((width, features), BF16),
            pltpu.VMEM((GROUPS, 2 * width, wide), BF16),
            pltpu.VMEM((GROUPS, rows, wide), F32),
            pltpu.VMEM((RING, blocks, cap, 2 * width), BF16),
            pltpu.VMEM((RING, blocks, cap, 2 * width), BF16),
            pltpu.VMEM((RING, blocks, cap, 2 * width), BF16),
            pltpu.VMEM((slots // 2, 2 * width), F32),
            pltpu.VMEM((slots // 2, 2 * width), F32),
            pltpu.VMEM((rows, 2 * width), BF16),
            pltpu.VMEM((n, cap, features), BF16),
            pltpu.VMEM((blocks, cap, 2 * width), BF16),
            pltpu.VMEM((CORES, RING, blocks, cap, 2 * width), BF16),
            pltpu.VMEM((adapters * width, rows), BF16),
            pltpu.VMEM((hops, chip_rows, wide), BF16),
            pltpu.VMEM((hops, chip_rows, wide), BF16),
            pltpu.VMEM((GROUPS, tok, wide), BF16),
            pltpu.VMEM((GROUPS, tok, wide), BF16),
            pltpu.VMEM((GROUPS, 2, CORES, tok, wide), BF16),
            pltpu.VMEM((slots, width), F32),
            pltpu.SemaphoreType.DMA((40,)),
            pltpu.SemaphoreType.DMA((40,)),
            pltpu.SemaphoreType.DMA((hops,)),
            pltpu.SemaphoreType.DMA((hops,)),
            pltpu.SemaphoreType.DMA((10,)),
            pltpu.SemaphoreType.DMA((10,)),
            pltpu.SemaphoreType.DMA((3,)),
            pltpu.SemaphoreType.DMA((3,)),
            pltpu.SemaphoreType.DMA((5,)),
            pltpu.SemaphoreType.DMA((4 * GROUPS,)),
            pltpu.SemaphoreType.DMA((4 * GROUPS,)),
        ],
        compiler_params=pltpu.CompilerParams(
            collective_id=0, has_side_effects=True, vmem_limit_bytes=54 * 1024 * 1024
        ),
    )(
        x,
        w,
        b,
        e.transpose(0, 2, 1).reshape(adapters * width, depth),
        sens,
        user_ids.reshape(blocks, LANES),
        slot_table[0],
        counts[0],
    )
    entry_grad = entry_grad.reshape(adapters, width, depth).transpose(0, 2, 1)
    return out[None], entry_grad[None], exit_grad[None, None]


def solution(mesh):
    in_specs = (
        P("mp", None, "dp"),
        P("dp", "mp"),
        P("mp", None, "dp", None),
        P("mp", "dp", None, None),
        P("mp", "dp", None),
        P("mp", None),
        P("mp", None),
        P("mp", None),
    )
    out_specs = (P("mp", "dp", None), P("mp", None, "dp", None), P("mp", "dp", None, None))
    return jax.shard_map(on_device, mesh=mesh, in_specs=in_specs, out_specs=out_specs, check_vma=False)
```

```python
import jax
import jax.numpy as jnp
from jax import lax
from jax.experimental import pallas as pl
from jax.experimental.pallas import tpu as pltpu
from jax.sharding import PartitionSpec as P

F32 = jnp.float32
BF16 = jnp.bfloat16
MESH = pl.DeviceIdType.MESH
SIDE = 4
RING = 8
CORES = 2
UP = (3, 4, 3, 4)
DOWN = (4, 3, 4, 3)
ORDER = [
    (0, 0), (1, 0), (3, 0), (0, 1),
    (0, 3), (1, 1), (3, 1), (1, 3),
    (3, 3), (2, 0), (0, 2), (1, 2),
    (2, 1), (2, 3), (3, 2), (2, 2),
]
GROUPS = 4
LANES = 128


def exchange(
    x_in, w_in, b_in, e_in, cotangent, users_in, table_in, counts_in,
    out_ref, exit_ref, entry_ref,
    x_ref, w_ref, b_ref, e_ref, sens_ref, users_ref, table_ref, counts_ref, owner_ref, slot_ref, column_ref, ranks_out, sens_out,
    x_sib, w_all, b_sib, b_all, y_all, rank_pair, pair_sum, rank_in, rank_own, rank_sib, rank_rows, sens_in, grad_out, grad_in, grad_rows,
    part_out, part_in, near_out, last_in, grad_sum,
    ag_send, ag_recv, rs_send, rs_recv, pair_send, pair_recv, all_send, all_recv, load, last_recv,
):
    n = RING * CORES
    dp = lax.axis_index("dp")
    mp = lax.axis_index("mp")
    z, c = dp // CORES, dp % CORES
    my_y, my_x = mp // SIDE, mp % SIDE
    sib = dp + 1 - 2 * c
    depth = w_ref.shape[0]
    half = depth // 2
    rows = x_ref.shape[0]
    chip_rows = rows // RING
    own_rows = chip_rows // CORES
    wide = LANES * (len(ORDER) // GROUPS)
    features = b_ref.shape[1]
    width = b_ref.shape[0]

    def at_x(sign):
        return my_y * SIDE + (my_x + SIDE + sign) % SIDE

    def at_y(sign):
        return ((my_y + SIDE + sign) % SIDE) * SIDE + my_x

    loads = [
        pltpu.make_async_copy(src, dst, load.at[k])
        for k, (src, dst) in enumerate(
            (
                (users_in, users_ref), (table_in, table_ref), (counts_in, counts_ref), (cotangent, sens_ref),
                (w_in, w_ref), (x_in, x_ref), (b_in, b_ref), (e_in, e_ref),
            )
        )
    ]
    for copy in loads:
        copy.start()

    barrier = pltpu.get_barrier_semaphore()
    for k in range(1, n):
        pl.semaphore_signal(barrier, inc=1, device_id={"dp": (dp + k) % n}, device_id_type=MESH)
    for to in (at_x(1), at_x(-1), at_y(1), at_y(-1)):
        pl.semaphore_signal(barrier, inc=1, device_id={"mp": to}, device_id_type=MESH)

    adapters = n
    seg = rows // n
    cap = seg // 8
    blocks = rows // LANES
    for copy in loads[0:3]:
        copy.wait()
    users = users_ref[...]
    line = lax.broadcasted_iota(jnp.int32, users.shape, 0)
    lane = lax.broadcasted_iota(jnp.int32, users.shape, 1)
    upper = lane >= seg
    storage = jnp.zeros_like(users)
    limit = jnp.zeros_like(users)
    for k in range(n):
        storage = jnp.where(users == k, table_ref[k], storage)
        limit = jnp.where((line == k // CORES) & (upper == bool(k % CORES)), counts_ref[k], limit)
    owner = jnp.where(jnp.where(upper, lane - seg, lane) < limit, storage, -1)
    ids = lax.broadcasted_iota(jnp.int32, (adapters, LANES), 0)
    hot = jnp.concatenate([jnp.where(owner[k : k + 1] == ids, 1.0, 0.0) for k in range(blocks)], axis=0)
    r0 = lax.broadcasted_iota(jnp.int32, (LANES, LANES), 0)
    r1 = lax.broadcasted_iota(jnp.int32, (LANES, LANES), 1)
    before_me = jnp.where((r0 < r1) & ((r0 >= seg) == (r1 >= seg)), 1.0, 0.0).astype(BF16)
    count = jnp.dot(hot.astype(BF16), before_me, preferred_element_type=F32)
    order = jnp.sum((hot * count).reshape(blocks, adapters, LANES), axis=1)
    slot = jnp.where(owner < 0, -1.0, owner.astype(F32) * cap + order)
    spot = order + (line * cap + jnp.where(upper, seg, 0)).astype(F32)
    column = jnp.where(owner == dp, spot, jnp.where(owner == sib, spot + LANES, -1.0))
    owner_ref[...] = owner
    slot_ref[...] = slot
    column_ref[...] = column
    slot_ids = lax.broadcasted_iota(jnp.int32, (LANES, LANES), 0).astype(F32)
    in_upper = r1 >= seg

    def pick(k):
        return jnp.where(slot_ref[pl.ds(k, 1), :] == slot_ids, 1.0, 0.0).astype(BF16)

    loads[3].wait()
    one_hot = jnp.where((slot_ref[pl.ds(z, 1), :] == slot_ids) & (in_upper == (c == 1)), 1.0, 0.0).astype(BF16)

    for i in range(features // wide):
        block = sens_ref[:, i * wide : (i + 1) * wide]
        chosen = jnp.dot(one_hot, jnp.concatenate([block, block], axis=0), preferred_element_type=F32)
        sens_out[:, :, i * wide : (i + 1) * wide] = chosen.reshape(n, cap, wide).astype(BF16)
    pl.semaphore_wait(barrier, n - 1 + 4)

    waits = []

    def send(src, dst, send_sem, recv_sem, to):
        copy = pltpu.make_async_remote_copy(
            src_ref=src, dst_ref=dst, send_sem=send_sem, recv_sem=recv_sem, device_id=to, device_id_type=MESH
        )
        copy.start()
        return copy

    def arrived(dst, sem):
        pltpu.make_async_copy(dst, dst, sem).wait()

    names = {}

    def sem_of(part, offset):
        return names.setdefault((part, offset), len(names))

    def place(part, offset, piece=None):
        spot = ORDER.index(offset)
        cols = pl.ds(LANES * (spot % GROUPS), LANES)
        if piece is None:
            return w_all.at[part * GROUPS + spot // GROUPS, :, cols]
        return w_all.at[part * GROUPS + spot // GROUPS, pl.ds(half * piece, half), cols]

    def pass_on(axis, sign, part, offset, piece=None, src=None):
        dx, dy = offset
        seen = ((dx - sign) % SIDE, dy) if axis == "x" else (dx, (dy - sign) % SIDE)
        to = at_x(sign) if axis == "x" else at_y(sign)
        if src is None:
            src = place(part, offset, piece)
        send_sem = ag_send.at[0 if piece is None else 1]
        send(src, place(part, seen, piece), send_sem, ag_recv.at[sem_of(part, seen)], {"mp": to})

    def got(part, offset):
        arrived(place(part, offset), ag_recv.at[sem_of(part, offset)])

    def both(axis, part, offset, src=None):
        for sign in (1, -1):
            pass_on(axis, sign, part, offset, None, src)

    def relay(axis, part, offset):
        away = offset[0] if axis == "x" else offset[1]
        if away == 1:
            pass_on(axis, -1, part, offset, 0)
        else:
            pass_on(axis, 1, part, offset, 1)

    def to_all(sem, src_of, dst, spans):
        def body(k, _):
            to = (dp + k) % n
            pltpu.make_async_remote_copy(
                src_ref=src_of(to), dst_ref=dst.at[dp], send_sem=all_send.at[sem], recv_sem=all_recv.at[sem],
                device_id={"dp": to}, device_id_type=MESH,
            ).start()
            return 0
        for first, last in spans:
            lax.fori_loop(first, last, body, 0)

    def to_chips(sem, src_of, dst):
        def body(k, _):
            to = (z + k) % RING
            pltpu.make_async_remote_copy(
                src_ref=src_of(to), dst_ref=dst, send_sem=all_send.at[sem], recv_sem=all_recv.at[sem],
                device_id={"dp": to * CORES + c}, device_id_type=MESH,
            ).start()
            return 0
        lax.fori_loop(1, RING, body, 0)

    to_all(1, lambda to: sens_out.at[to], sens_in, ((5, 7), (10, 12)))
    for copy in loads[4:7]:
        copy.wait()

    own_cols = w_ref.at[:, pl.ds(pl.multiple_of(LANES * c, LANES), LANES)]
    sib_cols = w_ref.at[:, pl.ds(pl.multiple_of(LANES * (1 - c), LANES), LANES)]
    waits.append(send(sib_cols, place(1, (0, 0)), pair_send.at[0], pair_recv.at[0], {"dp": sib}))
    both("x", 0, (0, 0), own_cols)
    waits.append(send(x_ref, x_sib, pair_send.at[1], pair_recv.at[1], {"dp": sib}))
    waits.append(send(b_ref, b_sib, pair_send.at[2], pair_recv.at[2], {"dp": sib}))
    w_all[0, :, 0:LANES] = own_cols[...]
    sens_in[dp] = sens_out[dp]
    arrived(place(1, (0, 0)), pair_recv.at[0])
    both("y", 1, (0, 0))
    both("y", 0, (0, 0), own_cols)
    both("x", 1, (0, 0))

    loads[7].wait()

    @pl.loop(0, blocks // 2)
    def _(i):
        tile = 2 * LANES
        every = lax.dot_general(
            e_ref[...], x_ref[pl.ds(pl.multiple_of(i * tile, tile), tile)], (((1,), (1,)), ((), ())),
            preferred_element_type=F32,
        )
        own = jnp.concatenate([owner_ref[pl.ds(2 * i, 1), :], owner_ref[pl.ds(2 * i + 1, 1), :]], axis=1)
        ranks = jnp.zeros((width, tile), F32)
        for k in range(adapters):
            ranks = ranks + jnp.where(own == k, every[k * width : (k + 1) * width], 0.0)
        for j in range(2):
            piece = ranks[:, j * LANES : (j + 1) * LANES]
            low = lax.broadcasted_iota(jnp.int32, piece.shape, 1) < seg
            spread = jnp.concatenate([jnp.where(low, piece, 0.0), jnp.where(low, 0.0, piece)], axis=0).astype(BF16)
            placed = lax.dot_general(pick(2 * i + j), spread, (((1,), (1,)), ((), ())), preferred_element_type=F32)
            placed = placed.reshape(RING, CORES, 1, cap, 2 * width).astype(BF16)
            for core in range(CORES):
                ranks_out[core, :, pl.ds(2 * i + j, 1)] = placed[:, core]

    waits.append(send(ranks_out.at[1 - c], rank_pair, pair_send.at[4], pair_recv.at[4], {"dp": sib}))
    arrived(rank_pair, pair_recv.at[4])
    pair_sum[...] = (ranks_out[c].astype(F32) + rank_pair[...].astype(F32)).astype(BF16)
    to_chips(0, lambda to: pair_sum.at[to], rank_in.at[z])
    to_all(1, lambda to: sens_out.at[to], sens_in, ((1, 5), (7, 8), (12, n)))
    rank_in[z] = pair_sum[z]

    for d in ((1, 0), (3, 0)):
        got(0, d)
        both("y", 0, d)
        relay("x", 0, d)
    for e in ((0, 1), (0, 3)):
        got(1, e)
        both("x", 1, e)
        relay("y", 1, e)

    for d in ((1, 0), (3, 0)):
        e = (d[1], d[0])
        got(1, d)
        relay("x", 1, d)
        got(0, e)
        relay("y", 0, e)

    arrived(b_sib, pair_recv.at[2])
    for g in range(GROUPS):
        for j in range(GROUPS):
            dx, dy = ORDER[g * GROUPS + j]
            m = ((my_y + dy) % SIDE) * SIDE + (my_x + dx) % SIDE
            col = pl.ds(pl.multiple_of(m * CORES * LANES + c * LANES, LANES), LANES)
            b_all[g, 0:width, j * LANES : (j + 1) * LANES] = b_ref[:, col]
            b_all[g, width : 2 * width, j * LANES : (j + 1) * LANES] = b_sib[:, col]
    arrived(rank_in.at[pl.ds(0, RING - 1)], all_recv.at[0])
    total = rank_in[0].astype(F32)
    for k in range(1, RING):
        total = total + rank_in[k].astype(F32)
    rank_own[...] = total.reshape(rank_own.shape)
    waits.append(send(rank_own, rank_sib, pair_send.at[3], pair_recv.at[3], {"dp": sib}))
    arrived(rank_sib, pair_recv.at[3])
    mine, theirs = rank_own[...], rank_sib[...]
    low = lax.broadcasted_iota(jnp.int32, mine.shape, 1) < width
    stack = jnp.concatenate(
        [
            jnp.where(low, mine, 0.0),
            jnp.where(low, pltpu.roll(mine, width, 1), 0.0),
            jnp.where(low, 0.0, pltpu.roll(theirs, width, 1)),
            jnp.where(low, 0.0, theirs),
        ],
        axis=0,
    ).astype(BF16)

    @pl.loop(0, blocks)
    def _(k):
        put = lax.broadcasted_iota(jnp.int32, (2 * LANES, LANES), 0).astype(F32) == column_ref[pl.ds(k, 1), :]
        put = jnp.where(put, 1.0, 0.0).astype(BF16)
        rank_rows[pl.ds(pl.multiple_of(k * LANES, LANES), LANES)] = lax.dot_general(
            put, stack, (((0,), (0,)), ((), ())), preferred_element_type=F32
        ).astype(BF16)

    arrived(x_sib, pair_recv.at[1])

    def product(g):
        tile = rows // 4

        @pl.loop(0, 4)
        def _(i):
            at = pl.ds(pl.multiple_of(i * tile, tile), tile)
            y_all[g, at] = (
                jnp.dot(x_ref[at], w_all[g], preferred_element_type=F32)
                + jnp.dot(x_sib[at], w_all[GROUPS + g], preferred_element_type=F32)
                + jnp.dot(rank_rows[at], b_all[g], preferred_element_type=F32)
            )

    def sem_rs(g, way, step):
        return g * (RING - 1) + (step - 1 if way > 0 else UP[g] + step - 1)

    def hop(g, step):
        for way, length in ((-1, DOWN[g]), (1, UP[g])):
            if step > length:
                continue
            dest = (z + RING + way * (length + 1 - step)) % RING
            value = y_all[g, pl.ds(pl.multiple_of(dest * chip_rows, chip_rows), chip_rows)]
            if step > 1:
                before = sem_rs(g, way, step - 1)
                arrived(part_in.at[before], rs_recv.at[before])
                value = value + part_in[before].astype(F32)
            num = sem_rs(g, way, step)
            part_out[num] = value.astype(BF16)
            to = ((z + RING + way) % RING) * CORES
            if step < length:
                send(part_out.at[num], part_in.at[num], rs_send.at[0], rs_recv.at[num], {"dp": to + c})
                continue
            side = (1 + way) // 2
            for core in range(CORES):
                piece = part_out.at[num, pl.ds(core * own_rows, own_rows)]
                send(piece, last_in.at[g, side * CORES + c], rs_send.at[0], last_recv.at[g], {"dp": to + core})

    def store(value, g, core):
        for j in range(GROUPS):
            dx, dy = ORDER[g * GROUPS + j]
            m = ((my_y + dy) % SIDE) * SIDE + (my_x + dx) % SIDE
            col = pl.ds(pl.multiple_of(m * CORES * LANES + core * LANES, LANES), LANES)
            out_ref[:, col] = value[:, j * LANES : (j + 1) * LANES]

    def rows_of(g, core):
        return y_all[g, pl.ds(pl.multiple_of(z * chip_rows + core * own_rows, own_rows), own_rows)]

    def lend(g):
        near_out[g] = rows_of(g, 1 - c).astype(BF16)
        send(near_out.at[g], last_in.at[g, 2 * CORES], rs_send.at[1], last_recv.at[g], {"dp": sib})

    def finish(g):
        arrived(last_in.at[g], last_recv.at[g])
        value = rows_of(g, c) + last_in[g, c].astype(F32) + last_in[g, CORES + c].astype(F32)
        store(value.astype(BF16), g, c)
        value = last_in[g, 2 * CORES].astype(F32)
        value = value + last_in[g, 1 - c].astype(F32) + last_in[g, CORES + 1 - c].astype(F32)
        store(value.astype(BF16), g, 1 - c)

    def exit_and_rank_gradients():
        arrived(sens_in.at[pl.ds(0, n - 1)], all_recv.at[1])
        mine = rank_own[...]
        halves = [mine[:, k * width : (k + 1) * width].reshape(blocks, 1, cap, width) for k in range(2)]
        ranks = jnp.concatenate(halves, axis=1).reshape(n * cap, width).astype(BF16)
        grad_sum[...] = jnp.zeros_like(grad_sum)

        @pl.loop(0, features // wide)
        def _(i):
            at = pl.ds(pl.multiple_of(i * wide, wide), wide)
            block = sens_in[:, :, at].astype(F32).reshape(n * cap, wide).astype(BF16)
            exit_ref[:, at] = lax.dot_general(ranks, block, (((0,), (0,)), ((), ())), preferred_element_type=F32)
            grad_sum[...] += lax.dot_general(
                block, b_ref[:, at], (((1,), (1,)), ((), ())), preferred_element_type=F32
            )

        grad = grad_sum[...].reshape(blocks, 2, cap, width)
        halves = [grad[:, k].reshape(blocks * cap, width) for k in range(2)]
        grad_out[...] = jnp.concatenate(halves, axis=1).reshape(blocks, cap, 2 * width).astype(BF16)
        to_chips(2, lambda to: grad_out, grad_in.at[c, z])
        grad_in[c, z] = grad_out[...]

    def swap_gradients():
        arrived(grad_in.at[0, pl.ds(0, RING - 1)], all_recv.at[2])
        waits.append(send(grad_in.at[c], grad_in.at[c], pair_send.at[5], pair_recv.at[5], {"dp": sib}))

    def spread_gradients():
        arrived(grad_in.at[0], pair_recv.at[5])

        @pl.loop(0, blocks)
        def _(k):
            block = jnp.concatenate([grad_in[core, :, pl.ds(k, 1)].astype(F32) for core in range(CORES)], axis=1)
            block = block.reshape(n * cap, 2 * width).astype(BF16)
            both_halves = lax.dot_general(block, pick(k), (((0,), (0,)), ((), ())), preferred_element_type=F32)
            low = lax.broadcasted_iota(jnp.int32, (width, LANES), 1) < seg
            grads = jnp.where(low, both_halves[0:width], both_halves[width : 2 * width])
            own = owner_ref[pl.ds(k, 1), :]
            at = pl.ds(pl.multiple_of(k * LANES, LANES), LANES)
            for u in range(adapters):
                grad_rows[u * width : (u + 1) * width, at] = jnp.where(own == u, grads, 0.0).astype(BF16)

    def entry_gradient(i):
        tile = adapters * width // 4
        at = slice(i * tile, (i + 1) * tile)
        entry_ref[at] = jnp.dot(grad_rows[at], x_ref[...], preferred_element_type=F32)

    def relay_both(d):
        got(1, d)
        relay("x", 1, d)
        e = (d[1], d[0])
        got(0, e)
        relay("y", 0, e)

    product(0)
    hop(0, 1)
    to_all(1, lambda to: sens_out.at[to], sens_in, ((8, 10),))
    for d in ((1, 1), (3, 1), (1, 3), (3, 3)):
        relay_both(d)
    hop(0, 2)
    got(0, (2, 0))
    both("y", 0, (2, 0))
    got(1, (0, 2))
    both("x", 1, (0, 2))
    product(1)
    hop(1, 1)
    lend(0)
    exit_and_rank_gradients()
    hop(0, 3)
    relay_both((1, 2))
    hop(1, 2)
    relay_both((3, 2))
    for part in (0, 1):
        for d in ((2, 0), (0, 2), (1, 2)):
            if (part, d) not in ((0, (2, 0)), (1, (0, 2)), (1, (1, 2))):
                got(part, d)
    product(2)
    hop(2, 1)
    for part in (0, 1):
        for d in ((2, 1), (2, 3), (3, 2), (2, 2)):
            if (part, d) not in ((0, (2, 1)), (0, (2, 3)), (1, (3, 2))):
                got(part, d)
    product(3)
    hop(3, 1)
    hop(0, 4)
    hop(1, 3)
    lend(1)
    lend(2)
    lend(3)
    hop(2, 2)
    swap_gradients()
    hop(3, 2)
    hop(1, 4)
    finish(0)
    hop(2, 3)
    spread_gradients()
    hop(3, 3)
    finish(1)
    entry_gradient(0)
    entry_gradient(1)
    hop(2, 4)
    entry_gradient(2)
    entry_gradient(3)
    hop(3, 4)
    for copy in waits:
        copy.wait_send()
    arrived(w_all.at[pl.ds(0, 5)], ag_send.at[0])
    arrived(w_all.at[pl.ds(0, 5), pl.ds(0, half)], ag_send.at[1])
    arrived(rank_in.at[pl.ds(0, RING - 1)], all_send.at[0])
    arrived(sens_in.at[pl.ds(0, n - 1)], all_send.at[1])
    arrived(rank_in.at[pl.ds(0, RING - 1)], all_send.at[2])
    arrived(near_out, rs_send.at[1])
    finish(2)
    finish(3)
    arrived(part_out, rs_send.at[0])


def store_results(out_vmem, exit_vmem, entry_vmem, out_ref, exit_ref, entry_ref, sem):
    copies = [
        pltpu.make_async_copy(src, dst, sem.at[k])
        for k, (src, dst) in enumerate(((entry_vmem, entry_ref), (exit_vmem, exit_ref), (out_vmem, out_ref)))
    ]
    for copy in copies:
        copy.start()
    for copy in copies:
        copy.wait()


def on_device(x, w, e, b, sens, user_ids, slot_table, counts):
    n = lax.axis_size("dp")
    x, e, b, sens = x[0], e[0], b[0, 0], sens[0]
    rows, depth = x.shape
    tok = rows // n
    cap = tok // 8
    adapters, _, width = e.shape
    features = b.shape[1]
    slots = n * cap
    blocks = rows // LANES
    wide = features // CORES // GROUPS
    hops = GROUPS * (RING - 1)
    chip_rows = rows // RING
    vmem = pl.BlockSpec(memory_space=pltpu.VMEM)
    out, exit_grad, entry_grad = pl.pallas_call(
        exchange,
        out_shape=(
            pltpu.VMEM((tok, features), BF16),
            pltpu.VMEM((width, features), F32),
            pltpu.VMEM((adapters * width, depth), F32),
        ),
        in_specs=[pl.BlockSpec(memory_space=pl.ANY)] * 8,
        out_specs=(vmem,) * 3,
        scratch_shapes=[
            pltpu.VMEM((rows, depth), BF16),
            pltpu.VMEM(w.shape, BF16),
            pltpu.VMEM((width, features), BF16),
            pltpu.VMEM((adapters * width, depth), BF16),
            pltpu.VMEM((tok, features), BF16),
            pltpu.VMEM((blocks, LANES), jnp.int32),
            pltpu.SMEM((adapters,), jnp.int32),
            pltpu.SMEM((n,), jnp.int32),
            pltpu.VMEM((blocks, LANES), jnp.int32),
            pltpu.VMEM((blocks, LANES), F32),
            pltpu.VMEM((blocks, LANES), F32),
            pltpu.VMEM((CORES, RING, blocks, cap, 2 * width), BF16),
            pltpu.VMEM((n, cap, features), BF16),
            pltpu.VMEM((rows, depth), BF16),
            pltpu.VMEM((2 * GROUPS, depth, wide), BF16),
            pltpu.VMEM((width, features), BF16),
            pltpu.VMEM((GROUPS, 2 * width, wide), BF16),
            pltpu.VMEM((GROUPS, rows, wide), F32),
            pltpu.VMEM((RING, blocks, cap, 2 * width), BF16),
            pltpu.VMEM((RING, blocks, cap, 2 * width), BF16),
            pltpu.VMEM((RING, blocks, cap, 2 * width), BF16),
            pltpu.VMEM((slots // 2, 2 * width), F32),
            pltpu.VMEM((slots // 2, 2 * width), F32),
            pltpu.VMEM((rows, 2 * width), BF16),
            pltpu.VMEM((n, cap, features), BF16),
            pltpu.VMEM((blocks, cap, 2 * width), BF16),
            pltpu.VMEM((CORES, RING, blocks, cap, 2 * width), BF16),
            pltpu.VMEM((adapters * width, rows), BF16),
            pltpu.VMEM((hops, chip_rows, wide), BF16),
            pltpu.VMEM((hops, chip_rows, wide), BF16),
            pltpu.VMEM((GROUPS, tok, wide), BF16),
            pltpu.VMEM((GROUPS, 2 * CORES + 1, tok, wide), BF16),
            pltpu.VMEM((slots, width), F32),
            pltpu.SemaphoreType.DMA((2,)),
            pltpu.SemaphoreType.DMA((2 * (len(ORDER) - 1),)),
            pltpu.SemaphoreType.DMA((2,)),
            pltpu.SemaphoreType.DMA((hops,)),
            pltpu.SemaphoreType.DMA((6,)),
            pltpu.SemaphoreType.DMA((6,)),
            pltpu.SemaphoreType.DMA((3,)),
            pltpu.SemaphoreType.DMA((3,)),
            pltpu.SemaphoreType.DMA((8,)),
            pltpu.SemaphoreType.DMA((GROUPS,)),
        ],
        compiler_params=pltpu.CompilerParams(
            collective_id=0, has_side_effects=True, vmem_limit_bytes=54 * 1024 * 1024
        ),
    )(
        x,
        w,
        b,
        e.transpose(0, 2, 1).reshape(adapters * width, depth),
        sens,
        user_ids.reshape(blocks, LANES),
        slot_table[0],
        counts[0],
    )
    anywhere = pl.BlockSpec(memory_space=pl.ANY)
    out, exit_grad, entry_grad = pl.pallas_call(
        store_results,
        out_shape=[jax.ShapeDtypeStruct(a.shape, a.dtype) for a in (out, exit_grad, entry_grad)],
        in_specs=[anywhere] * 3,
        out_specs=[anywhere] * 3,
        scratch_shapes=[pltpu.SemaphoreType.DMA((3,))],
        compiler_params=pltpu.CompilerParams(vmem_limit_bytes=1024 * 1024),
    )(out, exit_grad, entry_grad)
    entry_grad = entry_grad.reshape(adapters, width, depth).transpose(0, 2, 1)
    return out[None], entry_grad[None], exit_grad[None, None]


def solution(mesh):
    in_specs = (
        P("mp", None, "dp"),
        P("dp", "mp"),
        P("mp", None, "dp", None),
        P("mp", "dp", None, None),
        P("mp", "dp", None),
        P("mp", None),
        P("mp", None),
        P("mp", None),
    )
    out_specs = (P("mp", "dp", None), P("mp", None, "dp", None), P("mp", "dp", None, None))
    return jax.shard_map(on_device, mesh=mesh, in_specs=in_specs, out_specs=out_specs, check_vma=False)
```

```python
import jax
import jax.numpy as jnp
from jax import lax
from jax.experimental import pallas as pl
from jax.experimental.pallas import tpu as pltpu
from jax.sharding import PartitionSpec as P

F32 = jnp.float32
BF16 = jnp.bfloat16
MESH = pl.DeviceIdType.MESH
SIDE = 4
RING = 8
CORES = 2
UP = (3, 4, 3, 4)
DOWN = (4, 3, 4, 3)
ORDER = [
    (0, 0), (1, 0), (3, 0), (0, 1),
    (0, 3), (1, 1), (3, 1), (1, 3),
    (3, 3), (2, 0), (0, 2), (1, 2),
    (2, 1), (2, 3), (3, 2), (2, 2),
]
GROUPS = 4
LANES = 128


def exchange(
    x_in, w_in, b_in, e_in, cotangent, users_in, table_in, counts_in,
    out_ref, exit_ref, entry_ref,
    x_ref, w_ref, b_ref, e_ref, sens_ref, users_ref, table_ref, counts_ref, owner_ref, slot_ref, column_ref, ranks_out, sens_out,
    x_sib, w_all, b_sib, b_all, y_all, rank_pair, pair_sum, rank_in, rank_own, rank_sib, rank_rows, sens_in, grad_out, grad_in, grad_rows,
    part_out, part_in, near_out, last_in, grad_sum,
    ag_send, ag_recv, rs_send, rs_recv, pair_send, pair_recv, all_send, all_recv, load, last_recv,
):
    n = RING * CORES
    dp = lax.axis_index("dp")
    mp = lax.axis_index("mp")
    z, c = dp // CORES, dp % CORES
    my_y, my_x = mp // SIDE, mp % SIDE
    sib = dp + 1 - 2 * c
    depth = w_ref.shape[0]
    half = depth // 2
    rows = x_ref.shape[0]
    chip_rows = rows // RING
    own_rows = chip_rows // CORES
    wide = LANES * (len(ORDER) // GROUPS)
    features = b_ref.shape[1]
    width = b_ref.shape[0]

    def at_x(sign):
        return my_y * SIDE + (my_x + SIDE + sign) % SIDE

    def at_y(sign):
        return ((my_y + SIDE + sign) % SIDE) * SIDE + my_x

    loads = [
        pltpu.make_async_copy(src, dst, load.at[k])
        for k, (src, dst) in enumerate(
            (
                (users_in, users_ref), (table_in, table_ref), (counts_in, counts_ref), (cotangent, sens_ref),
                (w_in, w_ref), (x_in, x_ref), (b_in, b_ref), (e_in, e_ref),
            )
        )
    ]
    for copy in loads:
        copy.start()

    barrier = pltpu.get_barrier_semaphore()
    for k in range(1, n):
        pl.semaphore_signal(barrier, inc=1, device_id={"dp": (dp + k) % n}, device_id_type=MESH)
    for to in (at_x(1), at_x(-1), at_y(1), at_y(-1)):
        pl.semaphore_signal(barrier, inc=1, device_id={"mp": to}, device_id_type=MESH)

    adapters = n
    seg = rows // n
    cap = seg // 8
    blocks = rows // LANES
    for copy in loads[0:3]:
        copy.wait()
    users = users_ref[...]
    line = lax.broadcasted_iota(jnp.int32, users.shape, 0)
    lane = lax.broadcasted_iota(jnp.int32, users.shape, 1)
    upper = lane >= seg
    storage = jnp.zeros_like(users)
    limit = jnp.zeros_like(users)
    for k in range(n):
        storage = jnp.where(users == k, table_ref[k], storage)
        limit = jnp.where((line == k // CORES) & (upper == bool(k % CORES)), counts_ref[k], limit)
    owner = jnp.where(jnp.where(upper, lane - seg, lane) < limit, storage, -1)
    ids = lax.broadcasted_iota(jnp.int32, (adapters, LANES), 0)
    hot = jnp.concatenate([jnp.where(owner[k : k + 1] == ids, 1.0, 0.0) for k in range(blocks)], axis=0)
    r0 = lax.broadcasted_iota(jnp.int32, (LANES, LANES), 0)
    r1 = lax.broadcasted_iota(jnp.int32, (LANES, LANES), 1)
    before_me = jnp.where((r0 < r1) & ((r0 >= seg) == (r1 >= seg)), 1.0, 0.0).astype(BF16)
    count = jnp.dot(hot.astype(BF16), before_me, preferred_element_type=F32)
    order = jnp.sum((hot * count).reshape(blocks, adapters, LANES), axis=1)
    slot = jnp.where(owner < 0, -1.0, owner.astype(F32) * cap + order)
    spot = order + (line * cap + jnp.where(upper, seg, 0)).astype(F32)
    column = jnp.where(owner == dp, spot, jnp.where(owner == sib, spot + LANES, -1.0))
    owner_ref[...] = owner
    slot_ref[...] = slot
    column_ref[...] = column
    slot_ids = lax.broadcasted_iota(jnp.int32, (LANES, LANES), 0).astype(F32)
    in_upper = r1 >= seg

    def pick(k):
        return jnp.where(slot_ref[pl.ds(k, 1), :] == slot_ids, 1.0, 0.0).astype(BF16)

    loads[3].wait()
    one_hot = jnp.where((slot_ref[pl.ds(z, 1), :] == slot_ids) & (in_upper == (c == 1)), 1.0, 0.0).astype(BF16)

    for i in range(features // wide):
        block = sens_ref[:, i * wide : (i + 1) * wide]
        chosen = jnp.dot(one_hot, jnp.concatenate([block, block], axis=0), preferred_element_type=F32)
        sens_out[:, :, i * wide : (i + 1) * wide] = chosen.reshape(n, cap, wide).astype(BF16)
    pl.semaphore_wait(barrier, n - 1 + 4)

    waits = []

    def send(src, dst, send_sem, recv_sem, to):
        copy = pltpu.make_async_remote_copy(
            src_ref=src, dst_ref=dst, send_sem=send_sem, recv_sem=recv_sem, device_id=to, device_id_type=MESH
        )
        copy.start()
        return copy

    def arrived(dst, sem):
        pltpu.make_async_copy(dst, dst, sem).wait()

    names = {}

    def sem_of(part, offset):
        return names.setdefault((part, offset), len(names))

    def place(part, offset, piece=None):
        spot = ORDER.index(offset)
        cols = pl.ds(LANES * (spot % GROUPS), LANES)
        if piece is None:
            return w_all.at[part * GROUPS + spot // GROUPS, :, cols]
        return w_all.at[part * GROUPS + spot // GROUPS, pl.ds(half * piece, half), cols]

    def pass_on(axis, sign, part, offset, piece=None, src=None):
        dx, dy = offset
        seen = ((dx - sign) % SIDE, dy) if axis == "x" else (dx, (dy - sign) % SIDE)
        to = at_x(sign) if axis == "x" else at_y(sign)
        if src is None:
            src = place(part, offset, piece)
        send_sem = ag_send.at[0 if piece is None else 1]
        send(src, place(part, seen, piece), send_sem, ag_recv.at[sem_of(part, seen)], {"mp": to})

    def got(part, offset):
        arrived(place(part, offset), ag_recv.at[sem_of(part, offset)])

    def both(axis, part, offset, src=None):
        for sign in (1, -1):
            pass_on(axis, sign, part, offset, None, src)

    def relay(axis, part, offset):
        away = offset[0] if axis == "x" else offset[1]
        if away == 1:
            pass_on(axis, -1, part, offset, 0)
        else:
            pass_on(axis, 1, part, offset, 1)

    def to_all(sem, src_of, dst, spans):
        def body(k, _):
            to = (dp + k) % n
            pltpu.make_async_remote_copy(
                src_ref=src_of(to), dst_ref=dst.at[dp], send_sem=all_send.at[sem], recv_sem=all_recv.at[sem],
                device_id={"dp": to}, device_id_type=MESH,
            ).start()
            return 0
        for first, last in spans:
            lax.fori_loop(first, last, body, 0)

    def to_chips(sem, src_of, dst):
        def body(k, _):
            to = (z + k) % RING
            pltpu.make_async_remote_copy(
                src_ref=src_of(to), dst_ref=dst, send_sem=all_send.at[sem], recv_sem=all_recv.at[sem],
                device_id={"dp": to * CORES + c}, device_id_type=MESH,
            ).start()
            return 0
        lax.fori_loop(1, RING, body, 0)

    to_all(1, lambda to: sens_out.at[to], sens_in, ((5, 7), (10, 12)))
    for copy in loads[4:7]:
        copy.wait()

    own_cols = w_ref.at[:, pl.ds(pl.multiple_of(LANES * c, LANES), LANES)]
    sib_cols = w_ref.at[:, pl.ds(pl.multiple_of(LANES * (1 - c), LANES), LANES)]
    waits.append(send(sib_cols, place(1, (0, 0)), pair_send.at[0], pair_recv.at[0], {"dp": sib}))
    both("x", 0, (0, 0), own_cols)
    waits.append(send(x_ref, x_sib, pair_send.at[1], pair_recv.at[1], {"dp": sib}))
    waits.append(send(b_ref, b_sib, pair_send.at[2], pair_recv.at[2], {"dp": sib}))
    w_all[0, :, 0:LANES] = own_cols[...]
    sens_in[dp] = sens_out[dp]
    arrived(place(1, (0, 0)), pair_recv.at[0])
    both("y", 1, (0, 0))
    both("y", 0, (0, 0), own_cols)
    both("x", 1, (0, 0))

    loads[7].wait()

    @pl.loop(0, blocks // 2)
    def _(i):
        tile = 2 * LANES
        every = lax.dot_general(
            e_ref[...], x_ref[pl.ds(pl.multiple_of(i * tile, tile), tile)], (((1,), (1,)), ((), ())),
            preferred_element_type=F32,
        )
        own = jnp.concatenate([owner_ref[pl.ds(2 * i, 1), :], owner_ref[pl.ds(2 * i + 1, 1), :]], axis=1)
        ranks = jnp.zeros((width, tile), F32)
        for k in range(adapters):
            ranks = ranks + jnp.where(own == k, every[k * width : (k + 1) * width], 0.0)
        for j in range(2):
            piece = ranks[:, j * LANES : (j + 1) * LANES]
            low = lax.broadcasted_iota(jnp.int32, piece.shape, 1) < seg
            spread = jnp.concatenate([jnp.where(low, piece, 0.0), jnp.where(low, 0.0, piece)], axis=0).astype(BF16)
            placed = lax.dot_general(pick(2 * i + j), spread, (((1,), (1,)), ((), ())), preferred_element_type=F32)
            placed = placed.reshape(RING, CORES, 1, cap, 2 * width).astype(BF16)
            for core in range(CORES):
                ranks_out[core, :, pl.ds(2 * i + j, 1)] = placed[:, core]

    waits.append(send(ranks_out.at[1 - c], rank_pair, pair_send.at[4], pair_recv.at[4], {"dp": sib}))
    arrived(rank_pair, pair_recv.at[4])
    pair_sum[...] = (ranks_out[c].astype(F32) + rank_pair[...].astype(F32)).astype(BF16)
    to_chips(0, lambda to: pair_sum.at[to], rank_in.at[z])
    to_all(1, lambda to: sens_out.at[to], sens_in, ((1, 5), (7, 8), (12, n)))
    rank_in[z] = pair_sum[z]

    for d in ((1, 0), (3, 0)):
        got(0, d)
        both("y", 0, d)
        relay("x", 0, d)
    for e in ((0, 1), (0, 3)):
        got(1, e)
        both("x", 1, e)
        relay("y", 1, e)

    for d in ((1, 0), (3, 0)):
        e = (d[1], d[0])
        got(1, d)
        relay("x", 1, d)
        got(0, e)
        relay("y", 0, e)

    arrived(b_sib, pair_recv.at[2])
    for g in range(GROUPS):
        for j in range(GROUPS):
            dx, dy = ORDER[g * GROUPS + j]
            m = ((my_y + dy) % SIDE) * SIDE + (my_x + dx) % SIDE
            col = pl.ds(pl.multiple_of(m * CORES * LANES + c * LANES, LANES), LANES)
            b_all[g, 0:width, j * LANES : (j + 1) * LANES] = b_ref[:, col]
            b_all[g, width : 2 * width, j * LANES : (j + 1) * LANES] = b_sib[:, col]
    arrived(rank_in.at[pl.ds(0, RING - 1)], all_recv.at[0])
    total = rank_in[0].astype(F32)
    for k in range(1, RING):
        total = total + rank_in[k].astype(F32)
    rank_own[...] = total.reshape(rank_own.shape)
    waits.append(send(rank_own, rank_sib, pair_send.at[3], pair_recv.at[3], {"dp": sib}))
    arrived(rank_sib, pair_recv.at[3])
    mine, theirs = rank_own[...], rank_sib[...]
    low = lax.broadcasted_iota(jnp.int32, mine.shape, 1) < width
    stack = jnp.concatenate(
        [
            jnp.where(low, mine, 0.0),
            jnp.where(low, pltpu.roll(mine, width, 1), 0.0),
            jnp.where(low, 0.0, pltpu.roll(theirs, width, 1)),
            jnp.where(low, 0.0, theirs),
        ],
        axis=0,
    ).astype(BF16)

    @pl.loop(0, blocks)
    def _(k):
        put = lax.broadcasted_iota(jnp.int32, (2 * LANES, LANES), 0).astype(F32) == column_ref[pl.ds(k, 1), :]
        put = jnp.where(put, 1.0, 0.0).astype(BF16)
        rank_rows[pl.ds(pl.multiple_of(k * LANES, LANES), LANES)] = lax.dot_general(
            put, stack, (((0,), (0,)), ((), ())), preferred_element_type=F32
        ).astype(BF16)

    arrived(x_sib, pair_recv.at[1])

    def product(g):
        tile = rows // 4

        @pl.loop(0, 4)
        def _(i):
            at = pl.ds(pl.multiple_of(i * tile, tile), tile)
            y_all[g, at] = (
                jnp.dot(x_ref[at], w_all[g], preferred_element_type=F32)
                + jnp.dot(x_sib[at], w_all[GROUPS + g], preferred_element_type=F32)
                + jnp.dot(rank_rows[at], b_all[g], preferred_element_type=F32)
            )

    def sem_rs(g, way, step):
        return g * (RING - 1) + (step - 1 if way > 0 else UP[g] + step - 1)

    def hop(g, step):
        for way, length in ((-1, DOWN[g]), (1, UP[g])):
            if step > length:
                continue
            dest = (z + RING + way * (length + 1 - step)) % RING
            value = y_all[g, pl.ds(pl.multiple_of(dest * chip_rows, chip_rows), chip_rows)]
            if step > 1:
                before = sem_rs(g, way, step - 1)
                arrived(part_in.at[before], rs_recv.at[before])
                value = value + part_in[before].astype(F32)
            num = sem_rs(g, way, step)
            part_out[num] = value.astype(BF16)
            to = ((z + RING + way) % RING) * CORES
            if step < length:
                send(part_out.at[num], part_in.at[num], rs_send.at[0], rs_recv.at[num], {"dp": to + c})
                continue
            side = (1 + way) // 2
            for core in range(CORES):
                piece = part_out.at[num, pl.ds(core * own_rows, own_rows)]
                send(piece, last_in.at[g, side * CORES + c], rs_send.at[0], last_recv.at[g], {"dp": to + core})

    def store(value, g, core):
        for j in range(GROUPS):
            dx, dy = ORDER[g * GROUPS + j]
            m = ((my_y + dy) % SIDE) * SIDE + (my_x + dx) % SIDE
            col = pl.ds(pl.multiple_of(m * CORES * LANES + core * LANES, LANES), LANES)
            out_ref[:, col] = value[:, j * LANES : (j + 1) * LANES]

    def rows_of(g, core):
        return y_all[g, pl.ds(pl.multiple_of(z * chip_rows + core * own_rows, own_rows), own_rows)]

    def lend(g):
        near_out[g] = rows_of(g, 1 - c).astype(BF16)
        send(near_out.at[g], last_in.at[g, 2 * CORES], rs_send.at[1], last_recv.at[g], {"dp": sib})

    def finish(g):
        arrived(last_in.at[g], last_recv.at[g])
        value = rows_of(g, c) + last_in[g, c].astype(F32) + last_in[g, CORES + c].astype(F32)
        store(value.astype(BF16), g, c)
        value = last_in[g, 2 * CORES].astype(F32)
        value = value + last_in[g, 1 - c].astype(F32) + last_in[g, CORES + 1 - c].astype(F32)
        store(value.astype(BF16), g, 1 - c)

    def exit_and_rank_gradients():
        arrived(sens_in.at[pl.ds(0, n - 1)], all_recv.at[1])
        mine = rank_own[...]
        halves = [mine[:, k * width : (k + 1) * width].reshape(blocks, 1, cap, width) for k in range(2)]
        ranks = jnp.concatenate(halves, axis=1).reshape(n * cap, width).astype(BF16)
        grad_sum[...] = jnp.zeros_like(grad_sum)

        @pl.loop(0, features // wide)
        def _(i):
            at = pl.ds(pl.multiple_of(i * wide, wide), wide)
            block = sens_in[:, :, at].astype(F32).reshape(n * cap, wide).astype(BF16)
            exit_ref[:, at] = lax.dot_general(ranks, block, (((0,), (0,)), ((), ())), preferred_element_type=F32)
            grad_sum[...] += lax.dot_general(
                block, b_ref[:, at], (((1,), (1,)), ((), ())), preferred_element_type=F32
            )

        grad = grad_sum[...].reshape(blocks, 2, cap, width)
        halves = [grad[:, k].reshape(blocks * cap, width) for k in range(2)]
        grad_out[...] = jnp.concatenate(halves, axis=1).reshape(blocks, cap, 2 * width).astype(BF16)

    def send_gradients():
        to_chips(2, lambda to: grad_out, grad_in.at[c, z])
        grad_in[c, z] = grad_out[...]

    def swap_gradients():
        arrived(grad_in.at[0, pl.ds(0, RING - 1)], all_recv.at[2])
        waits.append(send(grad_in.at[c], grad_in.at[c], pair_send.at[5], pair_recv.at[5], {"dp": sib}))

    def spread_gradients():
        arrived(grad_in.at[0], pair_recv.at[5])

        @pl.loop(0, blocks)
        def _(k):
            block = jnp.concatenate([grad_in[core, :, pl.ds(k, 1)].astype(F32) for core in range(CORES)], axis=1)
            block = block.reshape(n * cap, 2 * width).astype(BF16)
            both_halves = lax.dot_general(block, pick(k), (((0,), (0,)), ((), ())), preferred_element_type=F32)
            low = lax.broadcasted_iota(jnp.int32, (width, LANES), 1) < seg
            grads = jnp.where(low, both_halves[0:width], both_halves[width : 2 * width])
            own = owner_ref[pl.ds(k, 1), :]
            at = pl.ds(pl.multiple_of(k * LANES, LANES), LANES)
            for u in range(adapters):
                grad_rows[u * width : (u + 1) * width, at] = jnp.where(own == u, grads, 0.0).astype(BF16)

    def entry_gradient(i):
        tile = adapters * width // 4
        at = slice(i * tile, (i + 1) * tile)
        entry_ref[at] = jnp.dot(grad_rows[at], x_ref[...], preferred_element_type=F32)

    def relay_both(d):
        got(1, d)
        relay("x", 1, d)
        e = (d[1], d[0])
        got(0, e)
        relay("y", 0, e)

    product(0)
    hop(0, 1)
    to_all(1, lambda to: sens_out.at[to], sens_in, ((8, 10),))
    for d in ((1, 1), (3, 1), (1, 3), (3, 3)):
        relay_both(d)
    hop(0, 2)
    got(0, (2, 0))
    both("y", 0, (2, 0))
    got(1, (0, 2))
    both("x", 1, (0, 2))
    product(1)
    hop(1, 1)
    lend(0)
    exit_and_rank_gradients()
    hop(0, 3)
    relay_both((1, 2))
    hop(1, 2)
    send_gradients()
    relay_both((3, 2))
    for part in (0, 1):
        for d in ((2, 0), (0, 2), (1, 2)):
            if (part, d) not in ((0, (2, 0)), (1, (0, 2)), (1, (1, 2))):
                got(part, d)
    product(2)
    hop(2, 1)
    for part in (0, 1):
        for d in ((2, 1), (2, 3), (3, 2), (2, 2)):
            if (part, d) not in ((0, (2, 1)), (0, (2, 3)), (1, (3, 2))):
                got(part, d)
    product(3)
    hop(3, 1)
    hop(1, 3)
    lend(1)
    lend(2)
    lend(3)
    hop(2, 2)
    swap_gradients()
    hop(3, 2)
    hop(0, 4)
    spread_gradients()
    entry_gradient(0)
    entry_gradient(1)
    hop(2, 3)
    hop(3, 3)
    hop(1, 4)
    finish(0)
    hop(2, 4)
    hop(3, 4)
    entry_gradient(2)
    entry_gradient(3)
    finish(1)
    for copy in waits:
        copy.wait_send()
    arrived(w_all.at[pl.ds(0, 5)], ag_send.at[0])
    arrived(w_all.at[pl.ds(0, 5), pl.ds(0, half)], ag_send.at[1])
    arrived(rank_in.at[pl.ds(0, RING - 1)], all_send.at[0])
    arrived(sens_in.at[pl.ds(0, n - 1)], all_send.at[1])
    arrived(rank_in.at[pl.ds(0, RING - 1)], all_send.at[2])
    arrived(near_out, rs_send.at[1])
    finish(2)
    finish(3)
    arrived(part_out, rs_send.at[0])


def store_results(out_vmem, exit_vmem, entry_vmem, out_ref, exit_ref, entry_ref, sem):
    copies = [
        pltpu.make_async_copy(src, dst, sem.at[k])
        for k, (src, dst) in enumerate(((entry_vmem, entry_ref), (exit_vmem, exit_ref), (out_vmem, out_ref)))
    ]
    for copy in copies:
        copy.start()
    for copy in copies:
        copy.wait()


def on_device(x, w, e, b, sens, user_ids, slot_table, counts):
    n = lax.axis_size("dp")
    x, e, b, sens = x[0], e[0], b[0, 0], sens[0]
    rows, depth = x.shape
    tok = rows // n
    cap = tok // 8
    adapters, _, width = e.shape
    features = b.shape[1]
    slots = n * cap
    blocks = rows // LANES
    wide = features // CORES // GROUPS
    hops = GROUPS * (RING - 1)
    chip_rows = rows // RING
    vmem = pl.BlockSpec(memory_space=pltpu.VMEM)
    out, exit_grad, entry_grad = pl.pallas_call(
        exchange,
        out_shape=(
            pltpu.VMEM((tok, features), BF16),
            pltpu.VMEM((width, features), F32),
            pltpu.VMEM((adapters * width, depth), F32),
        ),
        in_specs=[pl.BlockSpec(memory_space=pl.ANY)] * 8,
        out_specs=(vmem,) * 3,
        scratch_shapes=[
            pltpu.VMEM((rows, depth), BF16),
            pltpu.VMEM(w.shape, BF16),
            pltpu.VMEM((width, features), BF16),
            pltpu.VMEM((adapters * width, depth), BF16),
            pltpu.VMEM((tok, features), BF16),
            pltpu.VMEM((blocks, LANES), jnp.int32),
            pltpu.SMEM((adapters,), jnp.int32),
            pltpu.SMEM((n,), jnp.int32),
            pltpu.VMEM((blocks, LANES), jnp.int32),
            pltpu.VMEM((blocks, LANES), F32),
            pltpu.VMEM((blocks, LANES), F32),
            pltpu.VMEM((CORES, RING, blocks, cap, 2 * width), BF16),
            pltpu.VMEM((n, cap, features), BF16),
            pltpu.VMEM((rows, depth), BF16),
            pltpu.VMEM((2 * GROUPS, depth, wide), BF16),
            pltpu.VMEM((width, features), BF16),
            pltpu.VMEM((GROUPS, 2 * width, wide), BF16),
            pltpu.VMEM((GROUPS, rows, wide), F32),
            pltpu.VMEM((RING, blocks, cap, 2 * width), BF16),
            pltpu.VMEM((RING, blocks, cap, 2 * width), BF16),
            pltpu.VMEM((RING, blocks, cap, 2 * width), BF16),
            pltpu.VMEM((slots // 2, 2 * width), F32),
            pltpu.VMEM((slots // 2, 2 * width), F32),
            pltpu.VMEM((rows, 2 * width), BF16),
            pltpu.VMEM((n, cap, features), BF16),
            pltpu.VMEM((blocks, cap, 2 * width), BF16),
            pltpu.VMEM((CORES, RING, blocks, cap, 2 * width), BF16),
            pltpu.VMEM((adapters * width, rows), BF16),
            pltpu.VMEM((hops, chip_rows, wide), BF16),
            pltpu.VMEM((hops, chip_rows, wide), BF16),
            pltpu.VMEM((GROUPS, tok, wide), BF16),
            pltpu.VMEM((GROUPS, 2 * CORES + 1, tok, wide), BF16),
            pltpu.VMEM((slots, width), F32),
            pltpu.SemaphoreType.DMA((2,)),
            pltpu.SemaphoreType.DMA((2 * (len(ORDER) - 1),)),
            pltpu.SemaphoreType.DMA((2,)),
            pltpu.SemaphoreType.DMA((hops,)),
            pltpu.SemaphoreType.DMA((6,)),
            pltpu.SemaphoreType.DMA((6,)),
            pltpu.SemaphoreType.DMA((3,)),
            pltpu.SemaphoreType.DMA((3,)),
            pltpu.SemaphoreType.DMA((8,)),
            pltpu.SemaphoreType.DMA((GROUPS,)),
        ],
        compiler_params=pltpu.CompilerParams(
            collective_id=0, has_side_effects=True, vmem_limit_bytes=54 * 1024 * 1024
        ),
    )(
        x,
        w,
        b,
        e.transpose(0, 2, 1).reshape(adapters * width, depth),
        sens,
        user_ids.reshape(blocks, LANES),
        slot_table[0],
        counts[0],
    )
    anywhere = pl.BlockSpec(memory_space=pl.ANY)
    out, exit_grad, entry_grad = pl.pallas_call(
        store_results,
        out_shape=[jax.ShapeDtypeStruct(a.shape, a.dtype) for a in (out, exit_grad, entry_grad)],
        in_specs=[anywhere] * 3,
        out_specs=[anywhere] * 3,
        scratch_shapes=[pltpu.SemaphoreType.DMA((3,))],
        compiler_params=pltpu.CompilerParams(vmem_limit_bytes=1024 * 1024),
    )(out, exit_grad, entry_grad)
    entry_grad = entry_grad.reshape(adapters, width, depth).transpose(0, 2, 1)
    return out[None], entry_grad[None], exit_grad[None, None]


def solution(mesh):
    in_specs = (
        P("mp", None, "dp"),
        P("dp", "mp"),
        P("mp", None, "dp", None),
        P("mp", "dp", None, None),
        P("mp", "dp", None),
        P("mp", None),
        P("mp", None),
        P("mp", None),
    )
    out_specs = (P("mp", "dp", None), P("mp", None, "dp", None), P("mp", "dp", None, None))
    return jax.shard_map(on_device, mesh=mesh, in_specs=in_specs, out_specs=out_specs, check_vma=False)
```

```python
import jax
import jax.numpy as jnp
from jax import lax
from jax.experimental import pallas as pl
from jax.experimental.pallas import tpu as pltpu
from jax.sharding import PartitionSpec as P

F32 = jnp.float32
BF16 = jnp.bfloat16
MESH = pl.DeviceIdType.MESH
SIDE = 4
RING = 8
CORES = 2
UP = (3, 4, 3, 4)
DOWN = (4, 3, 4, 3)
ORDER = [
    (0, 0), (1, 0), (3, 0), (0, 1),
    (0, 3), (1, 1), (3, 1), (1, 3),
    (3, 3), (2, 0), (0, 2), (1, 2),
    (2, 1), (2, 3), (3, 2), (2, 2),
]
GROUPS = 4
LANES = 128


def exchange(
    x_in, w_in, b_in, e_in, cotangent, users_in, table_in, counts_in,
    out_ref, exit_ref, entry_ref,
    x_ref, w_ref, b_ref, e_ref, sens_ref, users_ref, table_ref, counts_ref, owner_ref, slot_ref, column_ref, ranks_out, sens_out,
    x_sib, w_all, b_sib, b_all, y_all, rank_pair, pair_sum, rank_in, rank_own, rank_sib, rank_rows, sens_in, grad_out, grad_in, grad_rows,
    part_out, part_in, near_out, last_in, grad_sum,
    ag_send, ag_recv, rs_send, rs_recv, pair_send, pair_recv, all_send, all_recv, load, last_recv,
):
    n = RING * CORES
    dp = lax.axis_index("dp")
    mp = lax.axis_index("mp")
    z, c = dp // CORES, dp % CORES
    my_y, my_x = mp // SIDE, mp % SIDE
    sib = dp + 1 - 2 * c
    depth = w_ref.shape[0]
    half = depth // 2
    rows = x_ref.shape[0]
    chip_rows = rows // RING
    own_rows = chip_rows // CORES
    wide = LANES * (len(ORDER) // GROUPS)
    features = b_ref.shape[1]
    width = b_ref.shape[0]

    def at_x(sign):
        return my_y * SIDE + (my_x + SIDE + sign) % SIDE

    def at_y(sign):
        return ((my_y + SIDE + sign) % SIDE) * SIDE + my_x

    loads = [
        pltpu.make_async_copy(src, dst, load.at[k])
        for k, (src, dst) in enumerate(
            (
                (users_in, users_ref), (table_in, table_ref), (counts_in, counts_ref), (cotangent, sens_ref),
                (w_in, w_ref), (x_in, x_ref), (b_in, b_ref), (e_in, e_ref),
            )
        )
    ]
    for copy in loads:
        copy.start()

    barrier = pltpu.get_barrier_semaphore()
    for k in range(1, n):
        pl.semaphore_signal(barrier, inc=1, device_id={"dp": (dp + k) % n}, device_id_type=MESH)
    for to in (at_x(1), at_x(-1), at_y(1), at_y(-1)):
        pl.semaphore_signal(barrier, inc=1, device_id={"mp": to}, device_id_type=MESH)

    adapters = n
    seg = rows // n
    cap = seg // 8
    blocks = rows // LANES
    for copy in loads[0:3]:
        copy.wait()
    users = users_ref[...]
    line = lax.broadcasted_iota(jnp.int32, users.shape, 0)
    lane = lax.broadcasted_iota(jnp.int32, users.shape, 1)
    upper = lane >= seg
    storage = jnp.zeros_like(users)
    limit = jnp.zeros_like(users)
    for k in range(n):
        storage = jnp.where(users == k, table_ref[k], storage)
        limit = jnp.where((line == k // CORES) & (upper == bool(k % CORES)), counts_ref[k], limit)
    owner = jnp.where(jnp.where(upper, lane - seg, lane) < limit, storage, -1)
    ids = lax.broadcasted_iota(jnp.int32, (adapters, LANES), 0)
    hot = jnp.concatenate([jnp.where(owner[k : k + 1] == ids, 1.0, 0.0) for k in range(blocks)], axis=0)
    r0 = lax.broadcasted_iota(jnp.int32, (LANES, LANES), 0)
    r1 = lax.broadcasted_iota(jnp.int32, (LANES, LANES), 1)
    before_me = jnp.where((r0 < r1) & ((r0 >= seg) == (r1 >= seg)), 1.0, 0.0).astype(BF16)
    count = jnp.dot(hot.astype(BF16), before_me, preferred_element_type=F32)
    order = jnp.sum((hot * count).reshape(blocks, adapters, LANES), axis=1)
    slot = jnp.where(owner < 0, -1.0, owner.astype(F32) * cap + order)
    spot = order + (line * cap + jnp.where(upper, seg, 0)).astype(F32)
    column = jnp.where(owner == dp, spot, jnp.where(owner == sib, spot + LANES, -1.0))
    owner_ref[...] = owner
    slot_ref[...] = slot
    column_ref[...] = column
    slot_ids = lax.broadcasted_iota(jnp.int32, (LANES, LANES), 0).astype(F32)
    in_upper = r1 >= seg

    def pick(k):
        return jnp.where(slot_ref[pl.ds(k, 1), :] == slot_ids, 1.0, 0.0).astype(BF16)

    loads[3].wait()
    one_hot = jnp.where((slot_ref[pl.ds(z, 1), :] == slot_ids) & (in_upper == (c == 1)), 1.0, 0.0).astype(BF16)

    for i in range(features // wide):
        block = sens_ref[:, i * wide : (i + 1) * wide]
        chosen = jnp.dot(one_hot, jnp.concatenate([block, block], axis=0), preferred_element_type=F32)
        sens_out[:, :, i * wide : (i + 1) * wide] = chosen.reshape(n, cap, wide).astype(BF16)
    pl.semaphore_wait(barrier, n - 1 + 4)

    waits = []

    def send(src, dst, send_sem, recv_sem, to):
        copy = pltpu.make_async_remote_copy(
            src_ref=src, dst_ref=dst, send_sem=send_sem, recv_sem=recv_sem, device_id=to, device_id_type=MESH
        )
        copy.start()
        return copy

    def arrived(dst, sem):
        pltpu.make_async_copy(dst, dst, sem).wait()

    names = {}

    def sem_of(part, offset):
        return names.setdefault((part, offset), len(names))

    def place(part, offset, piece=None):
        spot = ORDER.index(offset)
        cols = pl.ds(LANES * (spot % GROUPS), LANES)
        if piece is None:
            return w_all.at[part * GROUPS + spot // GROUPS, :, cols]
        return w_all.at[part * GROUPS + spot // GROUPS, pl.ds(half * piece, half), cols]

    def pass_on(axis, sign, part, offset, piece=None, src=None):
        dx, dy = offset
        seen = ((dx - sign) % SIDE, dy) if axis == "x" else (dx, (dy - sign) % SIDE)
        to = at_x(sign) if axis == "x" else at_y(sign)
        if src is None:
            src = place(part, offset, piece)
        send_sem = ag_send.at[0 if piece is None else 1]
        send(src, place(part, seen, piece), send_sem, ag_recv.at[sem_of(part, seen)], {"mp": to})

    def got(part, offset):
        arrived(place(part, offset), ag_recv.at[sem_of(part, offset)])

    def both(axis, part, offset, src=None):
        for sign in (1, -1):
            pass_on(axis, sign, part, offset, None, src)

    def relay(axis, part, offset):
        away = offset[0] if axis == "x" else offset[1]
        if away == 1:
            pass_on(axis, -1, part, offset, 0)
        else:
            pass_on(axis, 1, part, offset, 1)

    def to_all(sem, src_of, dst, spans):
        def body(k, _):
            to = (dp + k) % n
            pltpu.make_async_remote_copy(
                src_ref=src_of(to), dst_ref=dst.at[dp], send_sem=all_send.at[sem], recv_sem=all_recv.at[sem],
                device_id={"dp": to}, device_id_type=MESH,
            ).start()
            return 0
        for first, last in spans:
            lax.fori_loop(first, last, body, 0)

    def to_chips(sem, src_of, dst):
        def body(k, _):
            to = (z + k) % RING
            pltpu.make_async_remote_copy(
                src_ref=src_of(to), dst_ref=dst, send_sem=all_send.at[sem], recv_sem=all_recv.at[sem],
                device_id={"dp": to * CORES + c}, device_id_type=MESH,
            ).start()
            return 0
        lax.fori_loop(1, RING, body, 0)

    to_all(1, lambda to: sens_out.at[to], sens_in, ((5, 7), (10, 12)))
    for copy in loads[4:7]:
        copy.wait()

    own_cols = w_ref.at[:, pl.ds(pl.multiple_of(LANES * c, LANES), LANES)]
    sib_cols = w_ref.at[:, pl.ds(pl.multiple_of(LANES * (1 - c), LANES), LANES)]
    waits.append(send(sib_cols, place(1, (0, 0)), pair_send.at[0], pair_recv.at[0], {"dp": sib}))
    both("x", 0, (0, 0), own_cols)
    waits.append(send(x_ref, x_sib, pair_send.at[1], pair_recv.at[1], {"dp": sib}))
    waits.append(send(b_ref, b_sib, pair_send.at[2], pair_recv.at[2], {"dp": sib}))
    w_all[0, :, 0:LANES] = own_cols[...]
    sens_in[dp] = sens_out[dp]
    arrived(place(1, (0, 0)), pair_recv.at[0])
    both("y", 1, (0, 0))
    both("y", 0, (0, 0), own_cols)
    both("x", 1, (0, 0))

    loads[7].wait()

    @pl.loop(0, blocks // 2)
    def _(i):
        tile = 2 * LANES
        every = lax.dot_general(
            e_ref[...], x_ref[pl.ds(pl.multiple_of(i * tile, tile), tile)], (((1,), (1,)), ((), ())),
            preferred_element_type=F32,
        )
        own = jnp.concatenate([owner_ref[pl.ds(2 * i, 1), :], owner_ref[pl.ds(2 * i + 1, 1), :]], axis=1)
        ranks = jnp.zeros((width, tile), F32)
        for k in range(adapters):
            ranks = ranks + jnp.where(own == k, every[k * width : (k + 1) * width], 0.0)
        for j in range(2):
            piece = ranks[:, j * LANES : (j + 1) * LANES]
            low = lax.broadcasted_iota(jnp.int32, piece.shape, 1) < seg
            spread = jnp.concatenate([jnp.where(low, piece, 0.0), jnp.where(low, 0.0, piece)], axis=0).astype(BF16)
            placed = lax.dot_general(pick(2 * i + j), spread, (((1,), (1,)), ((), ())), preferred_element_type=F32)
            placed = placed.reshape(RING, CORES, 1, cap, 2 * width).astype(BF16)
            for core in range(CORES):
                ranks_out[core, :, pl.ds(2 * i + j, 1)] = placed[:, core]

    waits.append(send(ranks_out.at[1 - c], rank_pair, pair_send.at[4], pair_recv.at[4], {"dp": sib}))
    arrived(rank_pair, pair_recv.at[4])
    pair_sum[...] = (ranks_out[c].astype(F32) + rank_pair[...].astype(F32)).astype(BF16)
    to_chips(0, lambda to: pair_sum.at[to], rank_in.at[z])
    to_all(1, lambda to: sens_out.at[to], sens_in, ((1, 5), (7, 9), (12, n)))
    rank_in[z] = pair_sum[z]

    for d in ((1, 0), (3, 0)):
        got(0, d)
        both("y", 0, d)
        relay("x", 0, d)
    for e in ((0, 1), (0, 3)):
        got(1, e)
        both("x", 1, e)
        relay("y", 1, e)

    for d in ((1, 0), (3, 0)):
        e = (d[1], d[0])
        got(1, d)
        relay("x", 1, d)
        got(0, e)
        relay("y", 0, e)

    arrived(b_sib, pair_recv.at[2])
    for g in range(GROUPS):
        for j in range(GROUPS):
            dx, dy = ORDER[g * GROUPS + j]
            m = ((my_y + dy) % SIDE) * SIDE + (my_x + dx) % SIDE
            col = pl.ds(pl.multiple_of(m * CORES * LANES + c * LANES, LANES), LANES)
            b_all[g, 0:width, j * LANES : (j + 1) * LANES] = b_ref[:, col]
            b_all[g, width : 2 * width, j * LANES : (j + 1) * LANES] = b_sib[:, col]
    arrived(rank_in.at[pl.ds(0, RING - 1)], all_recv.at[0])
    total = rank_in[0].astype(F32)
    for k in range(1, RING):
        total = total + rank_in[k].astype(F32)
    rank_own[...] = total.reshape(rank_own.shape)
    waits.append(send(rank_own, rank_sib, pair_send.at[3], pair_recv.at[3], {"dp": sib}))
    arrived(rank_sib, pair_recv.at[3])
    mine, theirs = rank_own[...], rank_sib[...]
    low = lax.broadcasted_iota(jnp.int32, mine.shape, 1) < width
    stack = jnp.concatenate(
        [
            jnp.where(low, mine, 0.0),
            jnp.where(low, pltpu.roll(mine, width, 1), 0.0),
            jnp.where(low, 0.0, pltpu.roll(theirs, width, 1)),
            jnp.where(low, 0.0, theirs),
        ],
        axis=0,
    ).astype(BF16)

    @pl.loop(0, blocks)
    def _(k):
        put = lax.broadcasted_iota(jnp.int32, (2 * LANES, LANES), 0).astype(F32) == column_ref[pl.ds(k, 1), :]
        put = jnp.where(put, 1.0, 0.0).astype(BF16)
        rank_rows[pl.ds(pl.multiple_of(k * LANES, LANES), LANES)] = lax.dot_general(
            put, stack, (((0,), (0,)), ((), ())), preferred_element_type=F32
        ).astype(BF16)

    arrived(x_sib, pair_recv.at[1])

    def product(g):
        tile = rows // 4

        @pl.loop(0, 4)
        def _(i):
            at = pl.ds(pl.multiple_of(i * tile, tile), tile)
            y_all[g, at] = (
                jnp.dot(x_ref[at], w_all[g], preferred_element_type=F32)
                + jnp.dot(x_sib[at], w_all[GROUPS + g], preferred_element_type=F32)
                + jnp.dot(rank_rows[at], b_all[g], preferred_element_type=F32)
            )

    def sem_rs(g, way, step):
        return g * (RING - 1) + (step - 1 if way > 0 else UP[g] + step - 1)

    def landing(g, way, step):
        return g * (RING - 3) + (step - 1 if way > 0 else UP[g] + step - 2)

    def hop(g, step):
        for way, length in ((-1, DOWN[g]), (1, UP[g])):
            if step > length:
                continue
            dest = (z + RING + way * (length + 1 - step)) % RING
            value = y_all[g, pl.ds(pl.multiple_of(dest * chip_rows, chip_rows), chip_rows)]
            if step > 1:
                before = landing(g, way, step - 1)
                arrived(part_in.at[before], rs_recv.at[before])
                value = value + part_in[before].astype(F32)
            num = sem_rs(g, way, step)
            part_out[num] = value.astype(BF16)
            to = ((z + RING + way) % RING) * CORES
            if step < length:
                into = landing(g, way, step)
                send(part_out.at[num], part_in.at[into], rs_send.at[0], rs_recv.at[into], {"dp": to + c})
                continue
            side = (1 + way) // 2
            for core in range(CORES):
                piece = part_out.at[num, pl.ds(core * own_rows, own_rows)]
                send(piece, last_in.at[g, side * CORES + c], rs_send.at[0], last_recv.at[g], {"dp": to + core})

    def store(value, g, core):
        for j in range(GROUPS):
            dx, dy = ORDER[g * GROUPS + j]
            m = ((my_y + dy) % SIDE) * SIDE + (my_x + dx) % SIDE
            col = pl.ds(pl.multiple_of(m * CORES * LANES + core * LANES, LANES), LANES)
            out_ref[:, col] = value[:, j * LANES : (j + 1) * LANES]

    def rows_of(g, core):
        return y_all[g, pl.ds(pl.multiple_of(z * chip_rows + core * own_rows, own_rows), own_rows)]

    def lend(g):
        near_out[g] = rows_of(g, 1 - c).astype(BF16)
        send(near_out.at[g], last_in.at[g, 2 * CORES], rs_send.at[1], last_recv.at[g], {"dp": sib})

    def finish(g):
        arrived(last_in.at[g], last_recv.at[g])
        value = rows_of(g, c) + last_in[g, c].astype(F32) + last_in[g, CORES + c].astype(F32)
        store(value.astype(BF16), g, c)
        value = last_in[g, 2 * CORES].astype(F32)
        value = value + last_in[g, 1 - c].astype(F32) + last_in[g, CORES + 1 - c].astype(F32)
        store(value.astype(BF16), g, 1 - c)

    def exit_and_rank_gradients():
        arrived(sens_in.at[pl.ds(0, n - 1)], all_recv.at[1])
        mine = rank_own[...]
        halves = [mine[:, k * width : (k + 1) * width].reshape(blocks, 1, cap, width) for k in range(2)]
        ranks = jnp.concatenate(halves, axis=1).reshape(n * cap, width).astype(BF16)
        grad_sum[...] = jnp.zeros_like(grad_sum)

        @pl.loop(0, features // wide)
        def _(i):
            at = pl.ds(pl.multiple_of(i * wide, wide), wide)
            block = sens_in[:, :, at].astype(F32).reshape(n * cap, wide).astype(BF16)
            exit_ref[:, at] = lax.dot_general(ranks, block, (((0,), (0,)), ((), ())), preferred_element_type=F32)
            grad_sum[...] += lax.dot_general(
                block, b_ref[:, at], (((1,), (1,)), ((), ())), preferred_element_type=F32
            )

        grad = grad_sum[...].reshape(blocks, 2, cap, width)
        halves = [grad[:, k].reshape(blocks * cap, width) for k in range(2)]
        grad_out[...] = jnp.concatenate(halves, axis=1).reshape(blocks, cap, 2 * width).astype(BF16)

    def send_gradients():
        to_chips(2, lambda to: grad_out, grad_in.at[c, z])
        grad_in[c, z] = grad_out[...]

    def swap_gradients():
        arrived(grad_in.at[0, pl.ds(0, RING - 1)], all_recv.at[2])
        waits.append(send(grad_in.at[c], grad_in.at[c], pair_send.at[5], pair_recv.at[5], {"dp": sib}))

    def spread_gradients():
        arrived(grad_in.at[0], pair_recv.at[5])

        @pl.loop(0, blocks)
        def _(k):
            block = jnp.concatenate([grad_in[core, :, pl.ds(k, 1)].astype(F32) for core in range(CORES)], axis=1)
            block = block.reshape(n * cap, 2 * width).astype(BF16)
            both_halves = lax.dot_general(block, pick(k), (((0,), (0,)), ((), ())), preferred_element_type=F32)
            low = lax.broadcasted_iota(jnp.int32, (width, LANES), 1) < seg
            grads = jnp.where(low, both_halves[0:width], both_halves[width : 2 * width])
            own = owner_ref[pl.ds(k, 1), :]
            at = pl.ds(pl.multiple_of(k * LANES, LANES), LANES)
            for u in range(adapters):
                grad_rows[u * width : (u + 1) * width, at] = jnp.where(own == u, grads, 0.0).astype(BF16)

    def entry_gradient(i):
        tile = adapters * width // 4
        at = slice(i * tile, (i + 1) * tile)
        entry_ref[at] = jnp.dot(grad_rows[at], x_ref[...], preferred_element_type=F32)

    def relay_both(d):
        got(1, d)
        relay("x", 1, d)
        e = (d[1], d[0])
        got(0, e)
        relay("y", 0, e)

    product(0)
    hop(0, 1)
    to_all(1, lambda to: sens_out.at[to], sens_in, ((9, 10),))
    for d in ((1, 1), (3, 1), (1, 3), (3, 3)):
        relay_both(d)
    hop(0, 2)
    got(0, (2, 0))
    both("y", 0, (2, 0))
    got(1, (0, 2))
    both("x", 1, (0, 2))
    product(1)
    hop(1, 1)
    lend(0)
    exit_and_rank_gradients()
    hop(0, 3)
    relay_both((1, 2))
    hop(1, 2)
    send_gradients()
    relay_both((3, 2))
    for part in (0, 1):
        for d in ((2, 0), (0, 2), (1, 2)):
            if (part, d) not in ((0, (2, 0)), (1, (0, 2)), (1, (1, 2))):
                got(part, d)
    product(2)
    hop(2, 1)
    for part in (0, 1):
        for d in ((2, 1), (2, 3), (3, 2), (2, 2)):
            if (part, d) not in ((0, (2, 1)), (0, (2, 3)), (1, (3, 2))):
                got(part, d)
    product(3)
    hop(3, 1)
    hop(1, 3)
    lend(1)
    lend(2)
    lend(3)
    hop(2, 2)
    swap_gradients()
    hop(3, 2)
    hop(0, 4)
    spread_gradients()
    entry_gradient(0)
    entry_gradient(1)
    hop(2, 3)
    hop(3, 3)
    hop(1, 4)
    finish(0)
    hop(3, 4)
    hop(2, 4)
    entry_gradient(2)
    entry_gradient(3)
    finish(1)
    for copy in waits:
        copy.wait_send()
    arrived(w_all.at[pl.ds(0, 5)], ag_send.at[0])
    arrived(w_all.at[pl.ds(0, 5), pl.ds(0, half)], ag_send.at[1])
    arrived(rank_in.at[pl.ds(0, RING - 1)], all_send.at[0])
    arrived(sens_in.at[pl.ds(0, n - 1)], all_send.at[1])
    arrived(rank_in.at[pl.ds(0, RING - 1)], all_send.at[2])
    arrived(near_out, rs_send.at[1])
    finish(2)
    finish(3)
    arrived(part_out, rs_send.at[0])


def store_results(out_vmem, exit_vmem, entry_vmem, out_ref, exit_ref, entry_ref, sem):
    copies = [
        pltpu.make_async_copy(src, dst, sem.at[k])
        for k, (src, dst) in enumerate(((entry_vmem, entry_ref), (exit_vmem, exit_ref), (out_vmem, out_ref)))
    ]
    for copy in copies:
        copy.start()
    for copy in copies:
        copy.wait()


def on_device(x, w, e, b, sens, user_ids, slot_table, counts):
    n = lax.axis_size("dp")
    x, e, b, sens = x[0], e[0], b[0, 0], sens[0]
    rows, depth = x.shape
    tok = rows // n
    cap = tok // 8
    adapters, _, width = e.shape
    features = b.shape[1]
    slots = n * cap
    blocks = rows // LANES
    wide = features // CORES // GROUPS
    hops = GROUPS * (RING - 1)
    chip_rows = rows // RING
    vmem = pl.BlockSpec(memory_space=pltpu.VMEM)
    out, exit_grad, entry_grad = pl.pallas_call(
        exchange,
        out_shape=(
            pltpu.VMEM((tok, features), BF16),
            pltpu.VMEM((width, features), F32),
            pltpu.VMEM((adapters * width, depth), F32),
        ),
        in_specs=[pl.BlockSpec(memory_space=pl.ANY)] * 8,
        out_specs=(vmem,) * 3,
        scratch_shapes=[
            pltpu.VMEM((rows, depth), BF16),
            pltpu.VMEM(w.shape, BF16),
            pltpu.VMEM((width, features), BF16),
            pltpu.VMEM((adapters * width, depth), BF16),
            pltpu.VMEM((tok, features), BF16),
            pltpu.VMEM((blocks, LANES), jnp.int32),
            pltpu.SMEM((adapters,), jnp.int32),
            pltpu.SMEM((n,), jnp.int32),
            pltpu.VMEM((blocks, LANES), jnp.int32),
            pltpu.VMEM((blocks, LANES), F32),
            pltpu.VMEM((blocks, LANES), F32),
            pltpu.VMEM((CORES, RING, blocks, cap, 2 * width), BF16),
            pltpu.VMEM((n, cap, features), BF16),
            pltpu.VMEM((rows, depth), BF16),
            pltpu.VMEM((2 * GROUPS, depth, wide), BF16),
            pltpu.VMEM((width, features), BF16),
            pltpu.VMEM((GROUPS, 2 * width, wide), BF16),
            pltpu.VMEM((GROUPS, rows, wide), F32),
            pltpu.VMEM((RING, blocks, cap, 2 * width), BF16),
            pltpu.VMEM((RING, blocks, cap, 2 * width), BF16),
            pltpu.VMEM((RING, blocks, cap, 2 * width), BF16),
            pltpu.VMEM((slots // 2, 2 * width), F32),
            pltpu.VMEM((slots // 2, 2 * width), F32),
            pltpu.VMEM((rows, 2 * width), BF16),
            pltpu.VMEM((n, cap, features), BF16),
            pltpu.VMEM((blocks, cap, 2 * width), BF16),
            pltpu.VMEM((CORES, RING, blocks, cap, 2 * width), BF16),
            pltpu.VMEM((adapters * width, rows), BF16),
            pltpu.VMEM((hops, chip_rows, wide), BF16),
            pltpu.VMEM((GROUPS * (RING - 3), chip_rows, wide), BF16),
            pltpu.VMEM((GROUPS, tok, wide), BF16),
            pltpu.VMEM((GROUPS, 2 * CORES + 1, tok, wide), BF16),
            pltpu.VMEM((slots, width), F32),
            pltpu.SemaphoreType.DMA((2,)),
            pltpu.SemaphoreType.DMA((2 * (len(ORDER) - 1),)),
            pltpu.SemaphoreType.DMA((2,)),
            pltpu.SemaphoreType.DMA((GROUPS * (RING - 3),)),
            pltpu.SemaphoreType.DMA((6,)),
            pltpu.SemaphoreType.DMA((6,)),
            pltpu.SemaphoreType.DMA((3,)),
            pltpu.SemaphoreType.DMA((3,)),
            pltpu.SemaphoreType.DMA((8,)),
            pltpu.SemaphoreType.DMA((GROUPS,)),
        ],
        compiler_params=pltpu.CompilerParams(
            collective_id=0, has_side_effects=True, vmem_limit_bytes=54 * 1024 * 1024
        ),
    )(
        x,
        w,
        b,
        e.transpose(0, 2, 1).reshape(adapters * width, depth),
        sens,
        user_ids.reshape(blocks, LANES),
        slot_table[0],
        counts[0],
    )
    anywhere = pl.BlockSpec(memory_space=pl.ANY)
    out, exit_grad, entry_grad = pl.pallas_call(
        store_results,
        out_shape=[jax.ShapeDtypeStruct(a.shape, a.dtype) for a in (out, exit_grad, entry_grad)],
        in_specs=[anywhere] * 3,
        out_specs=[anywhere] * 3,
        scratch_shapes=[pltpu.SemaphoreType.DMA((3,))],
        compiler_params=pltpu.CompilerParams(vmem_limit_bytes=1024 * 1024),
    )(out, exit_grad, entry_grad)
    entry_grad = entry_grad.reshape(adapters, width, depth).transpose(0, 2, 1)
    return out[None], entry_grad[None], exit_grad[None, None]


def solution(mesh):
    in_specs = (
        P("mp", None, "dp"),
        P("dp", "mp"),
        P("mp", None, "dp", None),
        P("mp", "dp", None, None),
        P("mp", "dp", None),
        P("mp", None),
        P("mp", None),
        P("mp", None),
    )
    out_specs = (P("mp", "dp", None), P("mp", None, "dp", None), P("mp", "dp", None, None))
    return jax.shard_map(on_device, mesh=mesh, in_specs=in_specs, out_specs=out_specs, check_vma=False)
```

```python
import jax
import jax.numpy as jnp
from jax import lax
from jax.experimental import pallas as pl
from jax.experimental.pallas import tpu as pltpu
from jax.sharding import PartitionSpec as P

F32 = jnp.float32
BF16 = jnp.bfloat16
MESH = pl.DeviceIdType.MESH
SIDE = 4
RING = 8
CORES = 2
UP = (3, 4, 3, 4)
DOWN = (4, 3, 4, 3)
ORDER = [
    (0, 0), (1, 0), (3, 0), (0, 1),
    (0, 3), (1, 1), (3, 1), (1, 3),
    (3, 3), (2, 0), (0, 2), (1, 2),
    (2, 1), (2, 3), (3, 2), (2, 2),
]
GROUPS = 4
LANES = 128


def exchange(
    x_in, w_in, b_in, e_in, cotangent, users_in, table_in, counts_in,
    out_ref, exit_ref, entry_ref,
    x_ref, w_ref, b_ref, e_ref, sens_ref, users_ref, table_ref, counts_ref, owner_ref, slot_ref, column_ref, ranks_out, sens_out,
    x_sib, w_all, b_sib, b_all, y_all, rank_pair, pair_sum, rank_in, rank_own, rank_sib, rank_rows, sens_in, grad_out, grad_in, grad_rows,
    part_out, part_in, near_out, last_in, grad_sum,
    ag_send, ag_recv, rs_send, rs_recv, pair_send, pair_recv, all_send, all_recv, load, last_recv,
):
    n = RING * CORES
    dp = lax.axis_index("dp")
    mp = lax.axis_index("mp")
    z, c = dp // CORES, dp % CORES
    my_y, my_x = mp // SIDE, mp % SIDE
    sib = dp + 1 - 2 * c
    depth = w_ref.shape[0]
    half = depth // 2
    rows = x_ref.shape[0]
    chip_rows = rows // RING
    own_rows = chip_rows // CORES
    wide = LANES * (len(ORDER) // GROUPS)
    features = b_ref.shape[1]
    width = b_ref.shape[0]

    def at_x(sign):
        return my_y * SIDE + (my_x + SIDE + sign) % SIDE

    def at_y(sign):
        return ((my_y + SIDE + sign) % SIDE) * SIDE + my_x

    loads = [
        pltpu.make_async_copy(src, dst, load.at[k])
        for k, (src, dst) in enumerate(
            (
                (users_in, users_ref), (table_in, table_ref), (counts_in, counts_ref), (cotangent, sens_ref),
                (w_in, w_ref), (x_in, x_ref), (b_in, b_ref), (e_in, e_ref),
            )
        )
    ]
    for copy in loads:
        copy.start()

    barrier = pltpu.get_barrier_semaphore()
    for k in range(1, n):
        pl.semaphore_signal(barrier, inc=1, device_id={"dp": (dp + k) % n}, device_id_type=MESH)
    for to in (at_x(1), at_x(-1), at_y(1), at_y(-1)):
        pl.semaphore_signal(barrier, inc=1, device_id={"mp": to}, device_id_type=MESH)

    adapters = n
    seg = rows // n
    cap = seg // 8
    blocks = rows // LANES
    for copy in loads[0:3]:
        copy.wait()
    users = users_ref[...]
    line = lax.broadcasted_iota(jnp.int32, users.shape, 0)
    lane = lax.broadcasted_iota(jnp.int32, users.shape, 1)
    upper = lane >= seg
    storage = jnp.zeros_like(users)
    limit = jnp.zeros_like(users)
    for k in range(n):
        storage = jnp.where(users == k, table_ref[k], storage)
        limit = jnp.where((line == k // CORES) & (upper == bool(k % CORES)), counts_ref[k], limit)
    owner = jnp.where(jnp.where(upper, lane - seg, lane) < limit, storage, -1)
    ids = lax.broadcasted_iota(jnp.int32, (adapters, LANES), 0)
    hot = jnp.concatenate([jnp.where(owner[k : k + 1] == ids, 1.0, 0.0) for k in range(blocks)], axis=0)
    r0 = lax.broadcasted_iota(jnp.int32, (LANES, LANES), 0)
    r1 = lax.broadcasted_iota(jnp.int32, (LANES, LANES), 1)
    before_me = jnp.where((r0 < r1) & ((r0 >= seg) == (r1 >= seg)), 1.0, 0.0).astype(BF16)
    count = jnp.dot(hot.astype(BF16), before_me, preferred_element_type=F32)
    order = jnp.sum((hot * count).reshape(blocks, adapters, LANES), axis=1)
    slot = jnp.where(owner < 0, -1.0, owner.astype(F32) * cap + order)
    spot = order + (line * cap + jnp.where(upper, seg, 0)).astype(F32)
    column = jnp.where(owner == dp, spot, jnp.where(owner == sib, spot + LANES, -1.0))
    owner_ref[...] = owner
    slot_ref[...] = slot
    column_ref[...] = column
    slot_ids = lax.broadcasted_iota(jnp.int32, (LANES, LANES), 0).astype(F32)
    in_upper = r1 >= seg

    def pick(k):
        return jnp.where(slot_ref[pl.ds(k, 1), :] == slot_ids, 1.0, 0.0).astype(BF16)

    loads[3].wait()
    one_hot = jnp.where((slot_ref[pl.ds(z, 1), :] == slot_ids) & (in_upper == (c == 1)), 1.0, 0.0).astype(BF16)

    for i in range(features // wide):
        block = sens_ref[:, i * wide : (i + 1) * wide]
        chosen = jnp.dot(one_hot, jnp.concatenate([block, block], axis=0), preferred_element_type=F32)
        sens_out[:, :, i * wide : (i + 1) * wide] = chosen.reshape(n, cap, wide).astype(BF16)
    pl.semaphore_wait(barrier, n - 1 + 4)

    waits = []

    def send(src, dst, send_sem, recv_sem, to):
        copy = pltpu.make_async_remote_copy(
            src_ref=src, dst_ref=dst, send_sem=send_sem, recv_sem=recv_sem, device_id=to, device_id_type=MESH
        )
        copy.start()
        return copy

    def arrived(dst, sem):
        pltpu.make_async_copy(dst, dst, sem).wait()

    names = {}

    def sem_of(part, offset):
        return names.setdefault((part, offset), len(names))

    def place(part, offset, piece=None):
        spot = ORDER.index(offset)
        cols = pl.ds(LANES * (spot % GROUPS), LANES)
        if piece is None:
            return w_all.at[part * GROUPS + spot // GROUPS, :, cols]
        return w_all.at[part * GROUPS + spot // GROUPS, pl.ds(half * piece, half), cols]

    def pass_on(axis, sign, part, offset, piece=None, src=None):
        dx, dy = offset
        seen = ((dx - sign) % SIDE, dy) if axis == "x" else (dx, (dy - sign) % SIDE)
        to = at_x(sign) if axis == "x" else at_y(sign)
        if src is None:
            src = place(part, offset, piece)
        send_sem = ag_send.at[0 if piece is None else 1]
        send(src, place(part, seen, piece), send_sem, ag_recv.at[sem_of(part, seen)], {"mp": to})

    def got(part, offset):
        arrived(place(part, offset), ag_recv.at[sem_of(part, offset)])

    def both(axis, part, offset, src=None):
        for sign in (1, -1):
            pass_on(axis, sign, part, offset, None, src)

    def relay(axis, part, offset):
        away = offset[0] if axis == "x" else offset[1]
        if away == 1:
            pass_on(axis, -1, part, offset, 0)
        else:
            pass_on(axis, 1, part, offset, 1)

    def to_all(sem, src_of, dst, spans):
        def body(k, _):
            to = (dp + k) % n
            pltpu.make_async_remote_copy(
                src_ref=src_of(to), dst_ref=dst.at[dp], send_sem=all_send.at[sem], recv_sem=all_recv.at[sem],
                device_id={"dp": to}, device_id_type=MESH,
            ).start()
            return 0
        for first, last in spans:
            lax.fori_loop(first, last, body, 0)

    def to_chips(sem, src_of, dst):
        def body(k, _):
            to = (z + k) % RING
            pltpu.make_async_remote_copy(
                src_ref=src_of(to), dst_ref=dst, send_sem=all_send.at[sem], recv_sem=all_recv.at[sem],
                device_id={"dp": to * CORES + c}, device_id_type=MESH,
            ).start()
            return 0
        lax.fori_loop(1, RING, body, 0)

    to_all(1, lambda to: sens_out.at[to], sens_in, ((5, 7), (10, 12)))
    for copy in loads[4:7]:
        copy.wait()

    own_cols = w_ref.at[:, pl.ds(pl.multiple_of(LANES * c, LANES), LANES)]
    sib_cols = w_ref.at[:, pl.ds(pl.multiple_of(LANES * (1 - c), LANES), LANES)]
    waits.append(send(sib_cols, place(1, (0, 0)), pair_send.at[0], pair_recv.at[0], {"dp": sib}))
    both("x", 0, (0, 0), own_cols)
    waits.append(send(x_ref, x_sib, pair_send.at[1], pair_recv.at[1], {"dp": sib}))
    waits.append(send(b_ref, b_sib, pair_send.at[2], pair_recv.at[2], {"dp": sib}))
    w_all[0, :, 0:LANES] = own_cols[...]
    sens_in[dp] = sens_out[dp]
    arrived(place(1, (0, 0)), pair_recv.at[0])
    both("y", 1, (0, 0))
    both("y", 0, (0, 0), own_cols)
    both("x", 1, (0, 0))

    loads[7].wait()

    @pl.loop(0, blocks // 2)
    def _(i):
        tile = 2 * LANES
        every = lax.dot_general(
            e_ref[...], x_ref[pl.ds(pl.multiple_of(i * tile, tile), tile)], (((1,), (1,)), ((), ())),
            preferred_element_type=F32,
        )
        own = jnp.concatenate([owner_ref[pl.ds(2 * i, 1), :], owner_ref[pl.ds(2 * i + 1, 1), :]], axis=1)
        ranks = jnp.zeros((width, tile), F32)
        for k in range(adapters):
            ranks = ranks + jnp.where(own == k, every[k * width : (k + 1) * width], 0.0)
        for j in range(2):
            piece = ranks[:, j * LANES : (j + 1) * LANES]
            low = lax.broadcasted_iota(jnp.int32, piece.shape, 1) < seg
            spread = jnp.concatenate([jnp.where(low, piece, 0.0), jnp.where(low, 0.0, piece)], axis=0).astype(BF16)
            placed = lax.dot_general(pick(2 * i + j), spread, (((1,), (1,)), ((), ())), preferred_element_type=F32)
            placed = placed.reshape(RING, CORES, 1, cap, 2 * width).astype(BF16)
            for core in range(CORES):
                ranks_out[core, :, pl.ds(2 * i + j, 1)] = placed[:, core]

    waits.append(send(ranks_out.at[1 - c], rank_pair, pair_send.at[4], pair_recv.at[4], {"dp": sib}))
    arrived(rank_pair, pair_recv.at[4])
    pair_sum[...] = (ranks_out[c].astype(F32) + rank_pair[...].astype(F32)).astype(BF16)
    to_chips(0, lambda to: pair_sum.at[to], rank_in.at[z])
    to_all(1, lambda to: sens_out.at[to], sens_in, ((1, 5), (7, 9), (12, n)))
    rank_in[z] = pair_sum[z]

    for d in ((1, 0), (3, 0)):
        got(0, d)
        both("y", 0, d)
        relay("x", 0, d)
    for e in ((0, 1), (0, 3)):
        got(1, e)
        both("x", 1, e)
        relay("y", 1, e)

    for d in ((1, 0), (3, 0)):
        e = (d[1], d[0])
        got(1, d)
        relay("x", 1, d)
        got(0, e)
        relay("y", 0, e)

    arrived(b_sib, pair_recv.at[2])
    for g in range(GROUPS):
        for j in range(GROUPS):
            dx, dy = ORDER[g * GROUPS + j]
            m = ((my_y + dy) % SIDE) * SIDE + (my_x + dx) % SIDE
            col = pl.ds(pl.multiple_of(m * CORES * LANES + c * LANES, LANES), LANES)
            b_all[g, 0:width, j * LANES : (j + 1) * LANES] = b_ref[:, col]
            b_all[g, width : 2 * width, j * LANES : (j + 1) * LANES] = b_sib[:, col]
    arrived(rank_in.at[pl.ds(0, RING - 1)], all_recv.at[0])
    total = rank_in[0].astype(F32)
    for k in range(1, RING):
        total = total + rank_in[k].astype(F32)
    rank_own[...] = total.reshape(rank_own.shape)
    waits.append(send(rank_own, rank_sib, pair_send.at[3], pair_recv.at[3], {"dp": sib}))
    arrived(rank_sib, pair_recv.at[3])
    mine, theirs = rank_own[...], rank_sib[...]
    low = lax.broadcasted_iota(jnp.int32, mine.shape, 1) < width
    stack = jnp.concatenate(
        [
            jnp.where(low, mine, 0.0),
            jnp.where(low, pltpu.roll(mine, width, 1), 0.0),
            jnp.where(low, 0.0, pltpu.roll(theirs, width, 1)),
            jnp.where(low, 0.0, theirs),
        ],
        axis=0,
    ).astype(BF16)

    @pl.loop(0, blocks)
    def _(k):
        put = lax.broadcasted_iota(jnp.int32, (2 * LANES, LANES), 0).astype(F32) == column_ref[pl.ds(k, 1), :]
        put = jnp.where(put, 1.0, 0.0).astype(BF16)
        rank_rows[pl.ds(pl.multiple_of(k * LANES, LANES), LANES)] = lax.dot_general(
            put, stack, (((0,), (0,)), ((), ())), preferred_element_type=F32
        ).astype(BF16)

    arrived(x_sib, pair_recv.at[1])

    def product(g):
        tile = rows // 4

        @pl.loop(0, 4)
        def _(i):
            at = pl.ds(pl.multiple_of(i * tile, tile), tile)
            y_all[g, at] = (
                jnp.dot(x_ref[at], w_all[g], preferred_element_type=F32)
                + jnp.dot(x_sib[at], w_all[GROUPS + g], preferred_element_type=F32)
                + jnp.dot(rank_rows[at], b_all[g], preferred_element_type=F32)
            )

    def sem_rs(g, way, step):
        return g * (RING - 1) + (step - 1 if way > 0 else UP[g] + step - 1)

    def landing(g, way, step):
        return g * (RING - 3) + (step - 1 if way > 0 else UP[g] + step - 2)

    def hop(g, step):
        for way, length in ((-1, DOWN[g]), (1, UP[g])):
            if step > length:
                continue
            dest = (z + RING + way * (length + 1 - step)) % RING
            value = y_all[g, pl.ds(pl.multiple_of(dest * chip_rows, chip_rows), chip_rows)]
            if step > 1:
                before = landing(g, way, step - 1)
                arrived(part_in.at[before], rs_recv.at[before])
                value = value + part_in[before].astype(F32)
            num = sem_rs(g, way, step)
            part_out[num] = value.astype(BF16)
            to = ((z + RING + way) % RING) * CORES
            if step < length:
                into = landing(g, way, step)
                send(part_out.at[num], part_in.at[into], rs_send.at[0], rs_recv.at[into], {"dp": to + c})
                continue
            side = (1 + way) // 2
            for core in range(CORES):
                piece = part_out.at[num, pl.ds(core * own_rows, own_rows)]
                send(piece, last_in.at[g, side * CORES + c], rs_send.at[0], last_recv.at[g], {"dp": to + core})

    def store(value, g, core):
        for j in range(GROUPS):
            dx, dy = ORDER[g * GROUPS + j]
            m = ((my_y + dy) % SIDE) * SIDE + (my_x + dx) % SIDE
            col = pl.ds(pl.multiple_of(m * CORES * LANES + core * LANES, LANES), LANES)
            out_ref[:, col] = value[:, j * LANES : (j + 1) * LANES]

    def rows_of(g, core):
        return y_all[g, pl.ds(pl.multiple_of(z * chip_rows + core * own_rows, own_rows), own_rows)]

    def lend(g):
        near_out[g] = rows_of(g, 1 - c).astype(BF16)
        send(near_out.at[g], last_in.at[g, 2 * CORES], rs_send.at[1], last_recv.at[g], {"dp": sib})

    def finish(g):
        arrived(last_in.at[g], last_recv.at[g])
        value = rows_of(g, c) + last_in[g, c].astype(F32) + last_in[g, CORES + c].astype(F32)
        store(value.astype(BF16), g, c)
        value = last_in[g, 2 * CORES].astype(F32)
        value = value + last_in[g, 1 - c].astype(F32) + last_in[g, CORES + 1 - c].astype(F32)
        store(value.astype(BF16), g, 1 - c)

    def exit_and_rank_gradients():
        arrived(sens_in.at[pl.ds(0, n - 1)], all_recv.at[1])
        mine = rank_own[...]
        halves = [mine[:, k * width : (k + 1) * width].reshape(blocks, 1, cap, width) for k in range(2)]
        ranks = jnp.concatenate(halves, axis=1).reshape(n * cap, width).astype(BF16)
        grad_sum[...] = jnp.zeros_like(grad_sum)

        @pl.loop(0, features // wide)
        def _(i):
            at = pl.ds(pl.multiple_of(i * wide, wide), wide)
            block = sens_in[:, :, at].astype(F32).reshape(n * cap, wide).astype(BF16)
            exit_ref[:, at] = lax.dot_general(ranks, block, (((0,), (0,)), ((), ())), preferred_element_type=F32)
            grad_sum[...] += lax.dot_general(
                block, b_ref[:, at], (((1,), (1,)), ((), ())), preferred_element_type=F32
            )

        grad = grad_sum[...].reshape(blocks, 2, cap, width)
        halves = [grad[:, k].reshape(blocks * cap, width) for k in range(2)]
        grad_out[...] = jnp.concatenate(halves, axis=1).reshape(blocks, cap, 2 * width).astype(BF16)

    def send_gradients():
        to_chips(2, lambda to: grad_out, grad_in.at[c, z])
        grad_in[c, z] = grad_out[...]

    def swap_gradients():
        arrived(grad_in.at[0, pl.ds(0, RING - 1)], all_recv.at[2])
        waits.append(send(grad_in.at[c], grad_in.at[c], pair_send.at[5], pair_recv.at[5], {"dp": sib}))

    def spread_gradients():
        arrived(grad_in.at[0], pair_recv.at[5])

        @pl.loop(0, blocks)
        def _(k):
            block = jnp.concatenate([grad_in[core, :, pl.ds(k, 1)].astype(F32) for core in range(CORES)], axis=1)
            block = block.reshape(n * cap, 2 * width).astype(BF16)
            both_halves = lax.dot_general(block, pick(k), (((0,), (0,)), ((), ())), preferred_element_type=F32)
            low = lax.broadcasted_iota(jnp.int32, (width, LANES), 1) < seg
            grads = jnp.where(low, both_halves[0:width], both_halves[width : 2 * width])
            own = owner_ref[pl.ds(k, 1), :]
            at = pl.ds(pl.multiple_of(k * LANES, LANES), LANES)
            for u in range(adapters):
                grad_rows[u * width : (u + 1) * width, at] = jnp.where(own == u, grads, 0.0).astype(BF16)

    def entry_gradient(i):
        tile = adapters * width // 4
        at = slice(i * tile, (i + 1) * tile)
        entry_ref[at] = jnp.dot(grad_rows[at], x_ref[...], preferred_element_type=F32)

    def relay_both(d):
        got(1, d)
        relay("x", 1, d)
        e = (d[1], d[0])
        got(0, e)
        relay("y", 0, e)

    product(0)
    hop(0, 1)
    to_all(1, lambda to: sens_out.at[to], sens_in, ((9, 10),))
    for d in ((1, 1), (3, 1), (1, 3), (3, 3)):
        relay_both(d)
    hop(0, 2)
    got(0, (2, 0))
    both("y", 0, (2, 0))
    got(1, (0, 2))
    both("x", 1, (0, 2))
    product(1)
    hop(1, 1)
    lend(0)
    exit_and_rank_gradients()
    hop(0, 3)
    relay_both((1, 2))
    hop(1, 2)
    send_gradients()
    relay_both((3, 2))
    for part in (0, 1):
        for d in ((2, 0), (0, 2), (1, 2)):
            if (part, d) not in ((0, (2, 0)), (1, (0, 2)), (1, (1, 2))):
                got(part, d)
    product(2)
    hop(2, 1)
    for part in (0, 1):
        for d in ((2, 1), (2, 3), (3, 2), (2, 2)):
            if (part, d) not in ((0, (2, 1)), (0, (2, 3)), (1, (3, 2))):
                got(part, d)
    product(3)
    hop(3, 1)
    hop(1, 3)
    lend(1)
    lend(2)
    lend(3)
    hop(2, 2)
    swap_gradients()
    hop(3, 2)
    hop(0, 4)
    spread_gradients()
    entry_gradient(0)
    entry_gradient(1)
    hop(2, 3)
    hop(3, 3)
    hop(1, 4)
    hop(3, 4)
    hop(2, 4)
    entry_gradient(2)
    entry_gradient(3)
    finish(0)
    finish(1)
    for copy in waits:
        copy.wait_send()
    arrived(w_all.at[pl.ds(0, 5)], ag_send.at[0])
    arrived(w_all.at[pl.ds(0, 5), pl.ds(0, half)], ag_send.at[1])
    arrived(rank_in.at[pl.ds(0, RING - 1)], all_send.at[0])
    arrived(sens_in.at[pl.ds(0, n - 1)], all_send.at[1])
    arrived(rank_in.at[pl.ds(0, RING - 1)], all_send.at[2])
    arrived(near_out, rs_send.at[1])
    finish(2)
    finish(3)
    arrived(part_out, rs_send.at[0])


def store_results(out_vmem, exit_vmem, entry_vmem, out_ref, exit_ref, entry_ref, sem):
    copies = [
        pltpu.make_async_copy(src, dst, sem.at[k])
        for k, (src, dst) in enumerate(((entry_vmem, entry_ref), (exit_vmem, exit_ref), (out_vmem, out_ref)))
    ]
    for copy in copies:
        copy.start()
    for copy in copies:
        copy.wait()


def on_device(x, w, e, b, sens, user_ids, slot_table, counts):
    n = lax.axis_size("dp")
    x, e, b, sens = x[0], e[0], b[0, 0], sens[0]
    rows, depth = x.shape
    tok = rows // n
    cap = tok // 8
    adapters, _, width = e.shape
    features = b.shape[1]
    slots = n * cap
    blocks = rows // LANES
    wide = features // CORES // GROUPS
    hops = GROUPS * (RING - 1)
    chip_rows = rows // RING
    vmem = pl.BlockSpec(memory_space=pltpu.VMEM)
    out, exit_grad, entry_grad = pl.pallas_call(
        exchange,
        out_shape=(
            pltpu.VMEM((tok, features), BF16),
            pltpu.VMEM((width, features), F32),
            pltpu.VMEM((adapters * width, depth), F32),
        ),
        in_specs=[pl.BlockSpec(memory_space=pl.ANY)] * 8,
        out_specs=(vmem,) * 3,
        scratch_shapes=[
            pltpu.VMEM((rows, depth), BF16),
            pltpu.VMEM(w.shape, BF16),
            pltpu.VMEM((width, features), BF16),
            pltpu.VMEM((adapters * width, depth), BF16),
            pltpu.VMEM((tok, features), BF16),
            pltpu.VMEM((blocks, LANES), jnp.int32),
            pltpu.SMEM((adapters,), jnp.int32),
            pltpu.SMEM((n,), jnp.int32),
            pltpu.VMEM((blocks, LANES), jnp.int32),
            pltpu.VMEM((blocks, LANES), F32),
            pltpu.VMEM((blocks, LANES), F32),
            pltpu.VMEM((CORES, RING, blocks, cap, 2 * width), BF16),
            pltpu.VMEM((n, cap, features), BF16),
            pltpu.VMEM((rows, depth), BF16),
            pltpu.VMEM((2 * GROUPS, depth, wide), BF16),
            pltpu.VMEM((width, features), BF16),
            pltpu.VMEM((GROUPS, 2 * width, wide), BF16),
            pltpu.VMEM((GROUPS, rows, wide), F32),
            pltpu.VMEM((RING, blocks, cap, 2 * width), BF16),
            pltpu.VMEM((RING, blocks, cap, 2 * width), BF16),
            pltpu.VMEM((RING, blocks, cap, 2 * width), BF16),
            pltpu.VMEM((slots // 2, 2 * width), F32),
            pltpu.VMEM((slots // 2, 2 * width), F32),
            pltpu.VMEM((rows, 2 * width), BF16),
            pltpu.VMEM((n, cap, features), BF16),
            pltpu.VMEM((blocks, cap, 2 * width), BF16),
            pltpu.VMEM((CORES, RING, blocks, cap, 2 * width), BF16),
            pltpu.VMEM((adapters * width, rows), BF16),
            pltpu.VMEM((hops, chip_rows, wide), BF16),
            pltpu.VMEM((GROUPS * (RING - 3), chip_rows, wide), BF16),
            pltpu.VMEM((GROUPS, tok, wide), BF16),
            pltpu.VMEM((GROUPS, 2 * CORES + 1, tok, wide), BF16),
            pltpu.VMEM((slots, width), F32),
            pltpu.SemaphoreType.DMA((2,)),
            pltpu.SemaphoreType.DMA((2 * (len(ORDER) - 1),)),
            pltpu.SemaphoreType.DMA((2,)),
            pltpu.SemaphoreType.DMA((GROUPS * (RING - 3),)),
            pltpu.SemaphoreType.DMA((6,)),
            pltpu.SemaphoreType.DMA((6,)),
            pltpu.SemaphoreType.DMA((3,)),
            pltpu.SemaphoreType.DMA((3,)),
            pltpu.SemaphoreType.DMA((8,)),
            pltpu.SemaphoreType.DMA((GROUPS,)),
        ],
        compiler_params=pltpu.CompilerParams(
            collective_id=0, has_side_effects=True, vmem_limit_bytes=54 * 1024 * 1024
        ),
    )(
        x,
        w,
        b,
        e.transpose(0, 2, 1).reshape(adapters * width, depth),
        sens,
        user_ids.reshape(blocks, LANES),
        slot_table[0],
        counts[0],
    )
    anywhere = pl.BlockSpec(memory_space=pl.ANY)
    out, exit_grad, entry_grad = pl.pallas_call(
        store_results,
        out_shape=[jax.ShapeDtypeStruct(a.shape, a.dtype) for a in (out, exit_grad, entry_grad)],
        in_specs=[anywhere] * 3,
        out_specs=[anywhere] * 3,
        scratch_shapes=[pltpu.SemaphoreType.DMA((3,))],
        compiler_params=pltpu.CompilerParams(vmem_limit_bytes=1024 * 1024),
    )(out, exit_grad, entry_grad)
    entry_grad = entry_grad.reshape(adapters, width, depth).transpose(0, 2, 1)
    return out[None], entry_grad[None], exit_grad[None, None]


def solution(mesh):
    in_specs = (
        P("mp", None, "dp"),
        P("dp", "mp"),
        P("mp", None, "dp", None),
        P("mp", "dp", None, None),
        P("mp", "dp", None),
        P("mp", None),
        P("mp", None),
        P("mp", None),
    )
    out_specs = (P("mp", "dp", None), P("mp", None, "dp", None), P("mp", "dp", None, None))
    return jax.shard_map(on_device, mesh=mesh, in_specs=in_specs, out_specs=out_specs, check_vma=False)
```
